256 devices in a mesh: wide: 32 (over z_hi, x, core), narrow: 8 (over z_lo, y).
Axes of the slice: x: 4, y: 4, z: 8 (z_hi: 4, z_lo: 2; z = z_hi * 2 + z_lo), core: 2. Of those that a mesh axis runs over, the one named last changes fastest.
Arguments:
- three_index: bfloat16 [32, 3072, 1024], P('wide', None, 'narrow'), may hold values from -0.59765625 to 0.59765625
- orbital_map: int32 [32], replicated, may hold values from 0 to 31, each once
- occ_energy: float32 [32], replicated, may hold values from -2 to -0.3
- vir_energy: float32 [1024], replicated, may hold values from 0.2 to 3
- pair_kept: int32 [6, 32], P(None, 'wide'), may hold values 0 or 1
Outputs:
- density: float32 [32, 3072, 1024], P('wide', None, 'narrow')
The draws below stay inside these ranges and needn't reach their ends.
Inputs may be any that keep to these rules, and one draw needn't show every extreme that they name: `orbital_map`: each of the 32 orbitals once.
All inputs are finite; a program needn't handle non-finite values. No bound on the sum of `pair_kept` on one device may be relied on, other than what follows from the above.
Results may differ from the reference program's by a relative error of at most 0.0015.
Values may be sent and summed in bfloat16 or wider, within the bound.
A program may use at most 192 MiB of HBM per device.

```python
import jax
import jax.numpy as jnp
from jax import lax

NAUX = 3072
NVIR = 1024
OCC_DEV = 1
ROUNDS = 5
BLOCKS = 32
OCC = 32
N_WIDE = 32


def touch_ends(array, key, low, top_value):
    longest = array.shape.index(max(array.shape))
    spots = []
    for shift in (0, 1):
        where = [jax.random.randint(jax.random.fold_in(key, axis), (), 0, length) for axis, length in enumerate(array.shape)]
        where[longest] = (where[longest] + shift) % array.shape[longest]
        spots.append(tuple(where))
    return array.at[spots[0]].set(low).at[spots[1]].set(top_value)


def levels(rng, dims, split, least, high):
    level = 1.0
    for dim, parts in split:
        steps = jax.random.uniform(jax.random.fold_in(jax.random.fold_in(rng, 6), dim), (parts,), jnp.float32, least / len(split), high / len(split))
        level = level * jnp.repeat(jnp.exp(steps), dims[dim] // parts).reshape((-1,) + (1,) * (len(dims) - 1 - dim))
    return level


def scatter_about(key, dims, deviation, reach, split=(), kind=jnp.bfloat16):
    drawn = deviation * jax.random.normal(key, dims, jnp.float32)
    if split:
        drawn = drawn * levels(key, dims, split, -0.22, 0.18)
    return jnp.clip(drawn, -reach, reach).astype(kind)


def setup_inputs(seed: int = 0) -> dict:
    key_list = jax.random.split(jax.random.key(seed), 6)
    return {
        "three_index": scatter_about(key_list[0], (OCC, NAUX, NVIR), 0.1, 0.59765625, ((0, 32), (2, 8))),
        "orbital_map": jax.random.permutation(key_list[1], OCC).astype(jnp.int32),
        "occ_energy": jnp.clip(jax.random.uniform(key_list[2], (OCC,), jnp.float32, -2.0, -0.3), -2.0, -0.3),
        "vir_energy": jnp.clip(jax.random.uniform(key_list[3], (NVIR,), jnp.float32, 0.2, 3.0), 0.2, 3.0),
        "pair_kept": touch_ends((jax.random.randint(key_list[4], (ROUNDS + 1, BLOCKS), 0, 4) < 3).astype(jnp.int32), jax.random.fold_in(key_list[4], 1), 0, 1),
    }


def amplitudes(left, right, left_energy, right_energy, vir_energy, weight):
    coulomb = jnp.einsum("ipa,jpb->ijab", left.astype(jnp.float32), right.astype(jnp.float32))
    denominator = (vir_energy[:, None] + vir_energy[None, :])[None, None] - (left_energy[:, None] + right_energy[None, :])[:, :, None, None]
    rounded = lax.optimization_barrier((weight * coulomb / denominator).astype(jnp.bfloat16))
    return rounded.astype(jnp.float32)


def reference(three_index, orbital_map, occ_energy, vir_energy, pair_kept):
    blocks = three_index.reshape(N_WIDE, OCC_DEV, NAUX, NVIR)
    energies = occ_energy[orbital_map].reshape(N_WIDE, OCC_DEV)
    weights = pair_kept.astype(jnp.float32)

    def one_block(index):
        own_rows = blocks[index].astype(jnp.float32)
        own_energy = energies[index]
        forward = jnp.zeros((OCC_DEV, NAUX, NVIR), jnp.float32)
        for round_index in range(ROUNDS + 1):
            partner = (index - round_index) % N_WIDE
            right = blocks[partner].astype(jnp.float32)
            amplitude = amplitudes(own_rows, right, own_energy, energies[partner], vir_energy, weights[round_index, index])
            forward = forward + jnp.einsum("ijab,jpb->ipa", amplitude, right)
        backward = jnp.zeros((OCC_DEV, NAUX, NVIR), jnp.float32)
        for round_index in range(1, ROUNDS + 1):
            partner = (index + round_index) % N_WIDE
            left = blocks[partner].astype(jnp.float32)
            amplitude = amplitudes(left, own_rows, energies[partner], own_energy, vir_energy, weights[round_index, partner])
            backward = backward + jnp.einsum("ijab,ipa->jpb", amplitude, left)
        return forward + backward

    result = lax.map(one_block, jnp.arange(N_WIDE, dtype=jnp.int32))
    return result.reshape(N_WIDE * OCC_DEV, NAUX, NVIR)
```

```python
import functools

import jax
import jax.numpy as jnp
from jax import lax
from jax.experimental import pallas as pl
from jax.experimental.pallas import tpu as pltpu
from jax.sharding import PartitionSpec as P

MESH = pl.DeviceIdType.MESH
F32 = jnp.float32
BF16 = jnp.bfloat16

NX, NY, NZL = 4, 4, 2
EXTRA = 16
SLOTS = 12
LN2 = 0.6931471805599453
FINE = 64.0
TOP = 32000.0
COLUMN = (0, 1, 2, 4, 6, 3, 5, 7)
RELAY = True


def scale_of(level):
    return jnp.exp(level * (LN2 / FINE))


def encode(value, ref):
    rows = value.shape[0]
    top = jnp.maximum(jnp.max(jnp.abs(value), axis=0, keepdims=True), 1e-25)
    level = jnp.ceil(jnp.log(top) * (FINE / LN2))
    factor = TOP / scale_of(level)
    ref[0:rows, :] = jnp.round(value * factor).astype(jnp.int32).astype(jnp.int16)
    spread = jnp.broadcast_to(level, (EXTRA, value.shape[1]))
    ref[rows : rows + EXTRA, :] = spread.astype(jnp.int32).astype(jnp.int16)


def decode(ref, rows):
    level = ref[rows : rows + EXTRA, :].astype(jnp.int32).astype(F32)[0:1, :]
    return ref[0:rows, :].astype(jnp.int32).astype(F32) * (scale_of(level) * (1.0 / TOP))


def kernel(n_wide, naux, nloc, omap, occ, x, xt, kept, vir, out, bs, gt, va, tt, work, ss, rr, sz, rz,
           loc_sem, w_send, w_recv, s_send, s_recv, l_send, l_recv, g_send, g_recv, r_send, r_recv, z_send, z_recv):
    wide = lax.axis_index("wide")
    narrow = lax.axis_index("narrow")
    core = wide % 2
    chip = wide // 2
    cx = chip % NX
    zh8 = wide - wide % (2 * NX)
    zl, cy = narrow // NY, narrow % NY

    def around(by):
        return (wide + by + n_wide) % n_wide

    def ringx(by):
        return zh8 + ((cx + by + NX) % NX) * 2 + core

    up, down = (around(2), narrow), (around(-2), narrow)
    sib = (wide + 1 - 2 * core, narrow)
    right = (wide, zl * NY + (cy + 1) % NY)
    left = (wide, zl * NY + (cy + NY - 1) % NY)
    zpart = (wide, (1 - zl) * NY + cy)
    zup, zdown = (around(2 * NX), narrow), (around(-2 * NX), narrow)
    xup, xdown = (ringx(1), narrow), (ringx(-1), narrow)

    half = naux // 2
    h0, h1 = pl.ds(0, half), pl.ds(half, half + EXTRA)
    halves = (h0, h1)
    own = 4 + core
    other = 5 - core

    local = [
        pltpu.make_async_copy(x, bs.at[own, pl.ds(0, naux)], loc_sem.at[0]),
        pltpu.make_async_copy(kept, bs.at[own, pl.ds(naux, EXTRA)], loc_sem.at[1]),
        pltpu.make_async_copy(xt, gt.at[0], loc_sem.at[2]),
    ]
    for c in local:
        c.start()
    barrier = pltpu.get_barrier_semaphore()
    greeted = [up, down, sib, right, left, zpart, zup, zdown, xup, xdown]
    for device in greeted:
        pl.semaphore_signal(barrier, inc=1, device_id=device, device_id_type=MESH)
    pl.semaphore_wait(barrier, len(greeted))
    for c in local:
        c.wait()

    sent = []

    def send(src, dst, s_sem, r_sem, device):
        c = pltpu.make_async_remote_copy(src_ref=src, dst_ref=dst, send_sem=s_sem, recv_sem=r_sem,
                                         device_id=device, device_id_type=MESH)
        c.start()
        return c

    def arrived(dst, r_sem):
        pltpu.make_async_remote_copy(src_ref=dst, dst_ref=dst, send_sem=g_send.at[0], recv_sem=r_sem,
                                     device_id=sib, device_id_type=MESH).wait_recv()

    edge_up = cx == NX - 1
    edge_down = cx == 0

    def hop(message, src, slot, h, device, edge, over, relay):
        part = halves[h]
        if h == 1 and RELAY:
            to = (jnp.where(edge, over[0], device[0]), narrow)
            idx = jnp.where(edge, SLOTS + relay, slot)
            sent.append(send(bs.at[src, part], bs.at[idx, part], w_send.at[message, h], w_recv.at[idx, h], to))
        else:
            sent.append(send(bs.at[src, part], bs.at[slot, part], w_send.at[message, h], w_recv.at[slot, h], device))

    def hop_up(message, src, slot, h, relay):
        hop(message, src, slot, h, up, edge_up, zup, relay)

    def hop_down(message, src, slot, h, relay):
        hop(message, src, slot, h, down, edge_down, zdown, relay)

    def relayed(index, slot_up, slot_down, up_on, down_on):
        if not RELAY:
            return
        slot = jnp.where(edge_up, slot_up, slot_down)
        to = (jnp.where(edge_up, xup[0], xdown[0]), narrow)

        @pl.when(jnp.logical_or(jnp.logical_and(edge_up, up_on), jnp.logical_and(edge_down, down_on)))
        def _():
            arrived(bs.at[SLOTS + index, h1], w_recv.at[SLOTS + index, 1])
            send(bs.at[SLOTS + index, h1], bs.at[slot, h1], l_send.at[index], w_recv.at[slot, 1], to)

    def relay_done(index, up_on, down_on):
        if not RELAY:
            return

        @pl.when(jnp.logical_or(jnp.logical_and(edge_up, up_on), jnp.logical_and(edge_down, down_on)))
        def _():
            part = bs.at[SLOTS + index, h1]
            pltpu.make_async_remote_copy(src_ref=part, dst_ref=part, send_sem=l_send.at[index], recv_sem=w_recv.at[SLOTS + index, 1],
                                         device_id=sib, device_id_type=MESH).wait_send()

    def take(slot, h):
        arrived(bs.at[slot, halves[h]], w_recv.at[slot, h])

    def share(index, slot):
        sent.append(send(bs.at[slot], bs.at[slot], s_send.at[index], s_recv.at[slot], sib))

    def shared(slot):
        arrived(bs.at[slot], s_recv.at[slot])

    lo, hi = pl.ds(0, nloc // 2), pl.ds(nloc // 2, nloc // 2)

    sent.append(send(gt.at[0], gt.at[1], g_send.at[0], g_recv.at[1, 0], zpart))
    sent.append(send(gt.at[0], gt.at[3], g_send.at[1], g_recv.at[3, 0], right))
    sent.append(send(gt.at[0], gt.at[2], g_send.at[2], g_recv.at[2, 0], left))
    hop_up(0, own, 2 + core, 0, 0)
    hop_down(1, own, 6 + core, 0, 0)
    hop_up(0, own, 2 + core, 1, 0)
    hop_down(1, own, 6 + core, 1, 0)
    share(0, own)

    gy = (0, 0, 1, 3, 2, 1, 3, 2)
    gz = (0, 1, 0, 0, 0, 1, 1, 1)
    for g in range(8):
        row = vir[pl.ds(((zl + gz[g]) % NZL) * NY + (cy + gy[g]) % NY, 1), :]
        va[g] = jnp.broadcast_to(row, (nloc, nloc)).T
    vb = vir[pl.ds(narrow, 1), :]
    e_own = occ[omap[wide]]
    rows16 = lax.broadcasted_iota(jnp.int32, (EXTRA, nloc), 0)

    def block(q, g0, ng):
        pair = jnp.concatenate([bs[2 * q, 0:naux, :], bs[2 * q + 1, 0:naux, :]], axis=1)
        a = gt[g0 : g0 + ng].reshape(ng * nloc, naux)
        work[0 : ng * nloc, :] = jnp.dot(a, pair, preferred_element_type=F32)
        mine = bs[own, naux : naux + EXTRA, :].astype(F32)
        for k in range(2):
            j_off = jnp.where(q == 5, 6 - 11 * k, 2 * (q - 2) + k)
            e_sum = e_own + occ[omap[around(2 * chip - wide + j_off)]]
            delta = core - j_off
            theirs = bs[2 * q + k, naux : naux + EXTRA, :].astype(F32)
            pick = jnp.where(delta >= 0, mine, theirs)
            w = jnp.sum(jnp.where(rows16 == jnp.abs(delta), pick, 0.0), axis=0, keepdims=True)
            for g in range(g0, g0 + ng):
                v = work[(g - g0) * nloc : (g - g0 + 1) * nloc, k * nloc : (k + 1) * nloc]
                t = w * v / ((va[g] + vb) - e_sum)
                tt[pl.ds((2 * q + k) * nloc, nloc), COLUMN[g] * nloc : (COLUMN[g] + 1) * nloc] = t.T.astype(BF16)

    def blocks(first, count, stride, g0, ng):
        @pl.loop(0, count)
        def _(i):
            block(first + i * stride, g0, ng)

    shared(other)

    take(2 + core, 0)
    hop_up(2, 2 + core, core, 0, 1)
    take(6 + core, 0)
    hop_down(3, 6 + core, 8 + core, 0, 1)
    relayed(0, 2 + core, 6 + core, True, True)
    take(2 + core, 1)
    hop_up(2, 2 + core, core, 1, 1)
    share(1, 2 + core)
    take(6 + core, 1)
    hop_down(3, 6 + core, 8 + core, 1, 1)
    share(2, 6 + core)

    arrived(gt.at[3], g_recv.at[3, 0])
    sent.append(send(gt.at[3, lo], gt.at[4, lo], g_send.at[3], g_recv.at[4, 0], right))
    arrived(gt.at[2], g_recv.at[2, 0])
    sent.append(send(gt.at[2, hi], gt.at[4, hi], g_send.at[4], g_recv.at[4, 1], left))
    arrived(gt.at[1], g_recv.at[1, 0])
    sent.append(send(gt.at[1], gt.at[6], g_send.at[5], g_recv.at[6, 0], right))
    sent.append(send(gt.at[1], gt.at[5], g_send.at[6], g_recv.at[5, 0], left))

    shared(3 - core)
    shared(7 - core)
    blocks(1, 3, 1, 0, 4)

    third_src = 8 - 7 * core
    third_to = jnp.where(core == 0, down[0], up[0])
    third_over = jnp.where(core == 0, zdown[0], zup[0])
    third_edge = jnp.logical_or(jnp.logical_and(core == 0, edge_down), jnp.logical_and(core == 1, edge_up))
    take(core, 0)
    take(8 + core, 0)
    hop(4, third_src, 10 + core, 0, (third_to, narrow), third_edge, (third_over, narrow), 2)
    relayed(1, core, 8 + core, True, True)
    take(core, 1)
    take(8 + core, 1)
    hop(4, third_src, 10 + core, 1, (third_to, narrow), third_edge, (third_over, narrow), 2)
    share(3, core)
    share(4, 8 + core)

    arrived(gt.at[4, lo], g_recv.at[4, 0])
    arrived(gt.at[4, hi], g_recv.at[4, 1])
    shared(1 - core)
    shared(9 - core)
    blocks(1, 3, 1, 4, 1)

    arrived(gt.at[6], g_recv.at[6, 0])
    sent.append(send(gt.at[6, lo], gt.at[7, lo], g_send.at[7], g_recv.at[7, 0], right))
    arrived(gt.at[5], g_recv.at[5, 0])
    sent.append(send(gt.at[5, hi], gt.at[7, hi], g_send.at[8], g_recv.at[7, 1], left))
    blocks(0, 2, 4, 0, 7)
    relayed(2, 10 + core, 10 + core, core == 1, core == 0)
    take(10 + core, 0)
    take(10 + core, 1)
    share(5, 10 + core)
    blocks(1, 3, 1, 5, 2)
    shared(11 - core)
    blocks(5, 1, 1, 0, 7)
    arrived(gt.at[7, lo], g_recv.at[7, 0])
    arrived(gt.at[7, hi], g_recv.at[7, 1])
    blocks(0, 6, 1, 7, 1)

    quarter = naux // 4

    def tile(p, part):
        r0 = pl.multiple_of(part * quarter, quarter)
        lhs = jnp.concatenate([bs[s, pl.ds(r0, quarter), :] for s in range(SLOTS)], axis=1)
        cols = pl.ds(pl.multiple_of(p * 2 * nloc, 2 * nloc), 2 * nloc)
        work[0:quarter, :] = jnp.dot(lhs, tt[:, cols], preferred_element_type=F32)

    def y_copy(t):
        way, stage, j = t % 2, t // 4, (t % 4) // 2
        part = jnp.where(stage == 1, (1 - way) * 2 + j, way * 2 + j)
        slot = jnp.where(stage == 0, way * 2 + j, 4 + way * 4 + part)
        to = (wide, jnp.where(way == 0, right[1], left[1]))
        c = pltpu.make_async_remote_copy(src_ref=ss.at[t], dst_ref=rr.at[slot], send_sem=r_send.at[t], recv_sem=r_recv.at[slot],
                                         device_id=to, device_id_type=MESH)
        return c, way, stage, part, slot

    @pl.loop(0, 12)
    def _(t):
        c, way, stage, part, _ = y_copy(t)
        tile(jnp.where(stage == 0, 3, 1 + way), part)

        @pl.when(stage == 2)
        def _():
            arrived(rr.at[part], r_recv.at[part])
            work[0:quarter, :] += decode(rr.at[part], quarter)

        encode(work[0:quarter, :], ss.at[t])
        c.start()

    def z_copy(part):
        return pltpu.make_async_remote_copy(src_ref=sz.at[part], dst_ref=rz.at[part], send_sem=z_send.at[part], recv_sem=z_recv.at[part],
                                            device_id=zpart, device_id_type=MESH)

    @pl.loop(0, 4)
    def _(t):
        part = (t % 2) * 2 + t // 2
        tile(0, part)
        arrived(rr.at[4 + part], r_recv.at[4 + part])
        arrived(rr.at[8 + part], r_recv.at[8 + part])
        total = work[0:quarter, :] + decode(rr.at[4 + part], quarter) + decode(rr.at[8 + part], quarter)
        out[pl.ds(pl.multiple_of(part * quarter, quarter), quarter), :] = total[:, 0:nloc]
        encode(total[:, nloc : 2 * nloc], sz.at[part])
        z_copy(part).start()

    @pl.loop(0, 4)
    def _(t):
        part = (t % 2) * 2 + t // 2
        z_copy(part).wait_recv()
        out[pl.ds(pl.multiple_of(part * quarter, quarter), quarter), :] += decode(rz.at[part], quarter)

    for c in sent:
        c.wait_send()
    relay_done(0, True, True)
    relay_done(1, True, True)
    relay_done(2, core == 1, core == 0)

    @pl.loop(0, 12)
    def _(t):
        y_copy(t)[0].wait_send()

    @pl.loop(0, 4)
    def _(t):
        z_copy(t).wait_send()


def per_device(three_index, orbital_map, occ_energy, vir_energy, pair_kept):
    _, naux, nloc = three_index.shape
    n_wide = lax.axis_size("wide")
    n_narrow = lax.axis_size("narrow")
    x = three_index.reshape(naux, nloc)
    kept = jnp.pad(pair_kept, ((0, EXTRA - pair_kept.shape[0]), (0, 0))).astype(BF16)
    kept = jnp.broadcast_to(kept, (EXTRA, nloc))
    vir = vir_energy.reshape(n_narrow, nloc)
    quarter = naux // 4
    vmem = functools.partial(pl.BlockSpec, memory_space=pltpu.VMEM)
    smem = functools.partial(pl.BlockSpec, memory_space=pltpu.SMEM)
    hbm = functools.partial(pl.BlockSpec, memory_space=pl.ANY)
    dma = pltpu.SemaphoreType.DMA
    density = pl.pallas_call(
        functools.partial(kernel, n_wide, naux, nloc),
        out_shape=jax.ShapeDtypeStruct((naux, nloc), F32),
        in_specs=[smem(), smem(), hbm(), hbm(), hbm(), vmem()],
        out_specs=vmem(),
        scratch_shapes=[
            pltpu.VMEM((SLOTS + 3, naux + EXTRA, nloc), BF16),
            pltpu.VMEM((8, nloc, naux), BF16),
            pltpu.VMEM((8, nloc, nloc), F32),
            pltpu.VMEM((SLOTS * nloc, 8 * nloc), BF16),
            pltpu.VMEM((7 * nloc, 2 * nloc), F32),
            pltpu.VMEM((12, quarter + EXTRA, 2 * nloc), jnp.int16),
            pltpu.VMEM((12, quarter + EXTRA, 2 * nloc), jnp.int16),
            pltpu.VMEM((4, quarter + EXTRA, nloc), jnp.int16),
            pltpu.VMEM((4, quarter + EXTRA, nloc), jnp.int16),
            dma((3,)),
            dma((5, 2)),
            dma((SLOTS + 3, 2)),
            dma((6,)),
            dma((SLOTS,)),
            dma((3,)),
            dma((3,)),
            dma((9,)),
            dma((8, 2)),
            dma((12,)),
            dma((12,)),
            dma((4,)),
            dma((4,)),
        ],
        compiler_params=pltpu.CompilerParams(
            collective_id=0, has_side_effects=True, vmem_limit_bytes=60 * 1024 * 1024
        ),
    )(orbital_map, occ_energy, x, x.T, kept, vir)
    return density.reshape(1, naux, nloc)


def solution(mesh):
    placed = (P("wide", None, "narrow"), P(), P(), P(), P(None, "wide"))
    return jax.shard_map(
        per_device, mesh=mesh, in_specs=placed, out_specs=P("wide", None, "narrow"), check_vma=False
    )
```

```python
import functools
import heapq

import jax
import jax.numpy as jnp
from jax import lax
from jax.experimental import pallas as pl
from jax.experimental.pallas import tpu as pltpu
from jax.sharding import PartitionSpec as P

MESH = pl.DeviceIdType.MESH
F32 = jnp.float32
BF16 = jnp.bfloat16

NX, NY, NZL = 4, 4, 2
EXTRA = 16
SLOTS = 12
LN2 = 0.6931471805599453
FINE = 64.0
TOP = 32000.0
COLUMN = (0, 2, 4, 6, 1, 3, 5, 7)

HOP = 0.2
ROUTES = {
    (3, 1): ((3, ((3, 0), (0, 1), (3, 2))),),
    (3, 0): ((0, ((0, 1),)),),
    (2, 1): ((1, ((1, 0),)),),
    (2, 0): ((2, ((2, 1), (1, 0))),),
    (1, 1): ((1, ((1, 0),)), (0, ())),
}
ORDER = ((2, 3, 4, 5, 1, 0), (1, 2, 3, 4, 5, 0), (1, 2, 3, 0, 5, 4), (0, 1, 2, 5, 3, 4))
PHASES = ((3, 3), (4, 5), (5, 5), (5, 7), (6, 7), (6, 8))
RELAYS = 2


def slot_of(x, k, dz, owner):
    off = NX * dz + owner - x
    if -2 <= off <= 2:
        return 2 * (off + 2) + k
    if off == 3 and k == 0:
        return 10
    if off == -3 and k == 1:
        return 11
    return None


def messages():
    out = []

    def fw(k, xs, xd, dz, owner, h, rank=1):
        xs, xd, owner = xs % NX, xd % NX, owner % NX
        kind = "x+" if (xs + 1) % NX == xd else "x-"
        out.append((("S", dz, owner, h), kind, xs, xd, k, ("S", dz, owner, h), rank))

    for k in (0, 1):
        for x in range(NX):
            for h in (0, 1):
                fw(k, x, x + 1, 0, x, h, 2 + 0.1 * h)
                fw(k, x, x - 1, 0, x, 1 - h, 2 + 0.1 * h)
            fw(k, x + 1, x + 2, 0, x, 0)
            fw(k, x - 1, x - 2, 0, x, 1)
        for up in (True, False):
            kk, dz = (k, -1) if up else (1 - k, 1)

            def m(v, up=up):
                return v if up else NX - 1 - v

            for (owner, odd), ways in ROUTES.items():
                for h in (0, 1) if odd == k else ():
                    column, edges = ways[h * len(ways) // 2]
                    g = h if up else 1 - h
                    sent, got = ("S", 0, m(owner), g), ("S", dz, m(owner), g)
                    out.append((sent, "z+" if up else "z-", m(column), m(column), kk, got, 1))
                    for xs, xd in edges:
                        fw(kk, m(xs), m(xd), dz, m(owner), g, 0)
        for x in range(NX):

            def ag(g0, kind, g1, h, rank, k=k, x=x):
                out.append((("A", g0, h), kind, x, x, k, ("A", g1, h), rank))

            for h in (0, 1):
                ag(0, "zz", 4, h, 1 + 0.1 * h)
                ag(0, "y+", 2, h, 2 + 0.1 * h)
                ag(0, "y-", 1, 1 - h, 2 + 0.1 * h)
                ag(4, "y+", 6, h, 3)
                ag(4, "y-", 5, 1 - h, 3)
            ag(2, "y+", 3, 0, 1)
            ag(1, "y-", 3, 1, 1)
            ag(6, "y+", 7, 0, 1)
            ag(5, "y-", 7, 1, 1)
    return out


@functools.cache
def programs():
    ms = messages()
    need, free, heap = {}, {}, []
    ops = {(x, k): [] for x in range(NX) for k in (0, 1)}
    have, ready, late = {}, {}, {}

    def got(x, k, z, item, t):
        assert (x, k, z, item) not in late
        late[x, k, z, item] = t
        have[x, k, item] = max(have.get((x, k, item), 0.0), t)
        for i in need.get((x, k, item), ()):
            heapq.heappush(heap, (t, ms[i][6], i, z))

    for i, m in enumerate(ms):
        need.setdefault((m[2], m[4], m[0]), []).append(i)
    for x in range(NX):
        for k in (0, 1):
            for z in (0, 1):
                for h in (0, 1):
                    got(x, k, z, ("S", 0, x, h), 0.0)
                    got(x, k, z, ("A", 0, h), 0.0)
            ops[x, k].append((0.0, 9, 0, "share", 4 + k))
    while heap:
        t, rank, i, z = heapq.heappop(heap)
        _, kind, xs, xd, k, item2, _ = ms[i]
        if kind == "zz":
            links = [("even", z, xs)]
        elif kind in ("z+", "z-"):
            way = 0 if kind == "z+" else 1
            links = [("even", way, xs), ("odd", way, xs)]
        else:
            links = [(kind, xs, z)]
        start = max([t] + [free.get(link, 0.0) for link in links])
        for link in links:
            free[link] = start + 0.5
        ready[i] = max(ready.get(i, 0.0), t)
        got(xd, k, 1 - z if kind == "zz" else z, item2, start + 0.5 + HOP * len(links))
    for i, (item, kind, xs, xd, k, item2, rank) in enumerate(ms):
        ops[xs, k].append((ready[i], rank, i, "send", item, kind, xd, item2))
        ops[xd, k].append((have[xd, k, item2], -1, i, "wait", item2))
    for (x, k), program in ops.items():
        for dz in (-1, 0, 1):
            for owner in range(NX):
                both = [have.get((x, k, ("S", dz, owner, h))) for h in (0, 1)]
                slot = slot_of(x, k, dz, owner)
                if slot is not None and slot != 4 + k:
                    program.append((max(both), 1, 0, "share", slot))
        program.sort(key=lambda op: op[:3])
    return ops


@functools.cache
def phase_ends(x, k):
    ends, end = [], 0.01
    for pairs, slices in PHASES:
        slots = [2 * q + c for q in ORDER[x][:pairs] for c in (0, 1)]
        for core in (0, 1):
            for op in programs()[x, core]:
                if op[3] == "share" and op[4] in slots:
                    end = max(end, op[0])
                if op[3] == "wait" and op[4][0] == "A" and core == k and op[4][1] < slices:
                    end = max(end, op[0])
        ends.append(end)
    return [0.01, *ends, 1000.0]


def places(x, k):
    found, spare = {}, SLOTS
    for op in programs()[x, k]:
        if op[3] == "wait" and op[4][0] == "S" and op[4][:3] not in found:
            slot = slot_of(x, k, op[4][1], op[4][2])
            if slot is None:
                slot, spare = spare, spare + 1
            found[op[4][:3]] = slot
    found["S", 0, x] = 4 + k
    assert spare <= SLOTS + RELAYS
    return found


def scale_of(level):
    return jnp.exp(level * (LN2 / FINE))


def encode(value, ref):
    rows = value.shape[0]
    top = jnp.maximum(jnp.max(jnp.abs(value), axis=0, keepdims=True), 1e-25)
    level = jnp.ceil(jnp.log(top) * (FINE / LN2))
    factor = TOP / scale_of(level)
    ref[0:rows, :] = jnp.round(value * factor).astype(jnp.int32).astype(jnp.int16)
    spread = jnp.broadcast_to(level, (EXTRA, value.shape[1]))
    ref[rows : rows + EXTRA, :] = spread.astype(jnp.int32).astype(jnp.int16)


def decode(ref, rows):
    level = ref[rows : rows + EXTRA, :].astype(jnp.int32).astype(F32)[0:1, :]
    return ref[0:rows, :].astype(jnp.int32).astype(F32) * (scale_of(level) * (1.0 / TOP))


def kernel(n_wide, naux, nloc, omap, occ, x, xt, kept, vir, out, bs, gt, va, tt, work, keep, sy, ry, sn, rn,
           loc_sem, w_send, w_recv, s_send, s_recv, g_recv, sy_sem, ry_sem, sn_sem, rn_sem):
    wide = lax.axis_index("wide")
    narrow = lax.axis_index("narrow")
    core = wide % 2
    chip = wide // 2
    cx = chip % NX
    zh8 = wide - wide % (2 * NX)
    zl, cy = narrow // NY, narrow % NY

    def around(by):
        return (wide + by + n_wide) % n_wide

    def ringx(by):
        return zh8 + ((cx + by + NX) % NX) * 2 + core

    sib = (wide + 1 - 2 * core, narrow)
    right = (wide, zl * NY + (cy + 1) % NY)
    left = (wide, zl * NY + (cy + NY - 1) % NY)
    zpart = (wide, (1 - zl) * NY + cy)
    zup, zdown = (around(2 * NX), narrow), (around(-2 * NX), narrow)
    xup, xdown = (ringx(1), narrow), (ringx(-1), narrow)
    to = {"x+": xup, "x-": xdown, "z+": zup, "z-": zdown, "zz": zpart, "y+": right, "y-": left}

    half = naux // 2
    halves = (pl.ds(0, half), pl.ds(half, half + EXTRA))
    lo_hi = (pl.ds(0, nloc // 2), pl.ds(nloc // 2, nloc // 2))
    own = 4 + core

    local = [
        pltpu.make_async_copy(x, bs.at[own, pl.ds(0, naux)], loc_sem.at[0]),
        pltpu.make_async_copy(kept, bs.at[own, pl.ds(naux, EXTRA)], loc_sem.at[1]),
        pltpu.make_async_copy(xt, gt.at[0], loc_sem.at[2]),
    ]
    for c in local:
        c.start()
    barrier = pltpu.get_barrier_semaphore()
    greeted = [sib, *to.values()]
    for device in greeted:
        pl.semaphore_signal(barrier, inc=1, device_id=device, device_id_type=MESH)
    pl.semaphore_wait(barrier, len(greeted))
    for c in local:
        c.wait()

    def remote(src, dst, s_sem, r_sem, device):
        return pltpu.make_async_remote_copy(src_ref=src, dst_ref=dst, send_sem=s_sem, recv_sem=r_sem,
                                            device_id=device, device_id_type=MESH)

    def arrived(dst, r_sem):
        remote(dst, dst, w_send.at[0], r_sem, sib).wait_recv()

    def view(item, place):
        if item[0] == "S":
            slot, h = place[item[:3]], item[3]
            return bs.at[slot, halves[h]], w_recv.at[slot, h]
        return gt.at[item[1], lo_hi[item[2]]], g_recv.at[item[1], item[2]]

    def run(phase, finish=False):
        for x in range(NX):
            for k in (0, 1):

                @pl.when(jnp.logical_and(cx == x, core == k))
                def _(x=x, k=k):
                    place, n_sent, n_shared = places(x, k), 0, 0
                    ends = [-1.0, *phase_ends(x, k)]
                    for op in programs()[x, k]:
                        now = not finish and ends[phase] < op[0] <= ends[phase + 1]
                        if op[3] == "wait":
                            if now:
                                arrived(*view(op[4], place))
                        elif op[3] == "share":
                            part = bs.at[op[4]]
                            if now:
                                remote(part, part, s_send.at[n_shared], s_recv.at[op[4]], sib).start()
                            if finish:
                                remote(part, part, s_send.at[n_shared], s_recv.at[op[4]], sib).wait_send()
                            n_shared += 1
                        else:
                            _, _, _, _, item, kind, xd, there = op
                            dst, r_sem = view(there, places(xd, k))
                            if now:
                                remote(view(item, place)[0], dst, w_send.at[n_sent], r_sem, to[kind]).start()
                            if finish:
                                remote(view(item, place)[0], dst, w_send.at[n_sent], r_sem, to[kind]).wait_send()
                            n_sent += 1

    def shared(slot):
        arrived(bs.at[slot], s_recv.at[slot])

    run(0)

    gy = (0, 1, 3, 2) * 2
    gz = (0,) * 4 + (1,) * 4
    for g in range(8):
        row = vir[pl.ds(((zl + gz[g]) % NZL) * NY + (cy + gy[g]) % NY, 1), :]
        va[g] = jnp.broadcast_to(row, (nloc, nloc)).T
    vb = vir[pl.ds(narrow, 1), :]
    e_own = occ[omap[wide]]
    rows16 = lax.broadcasted_iota(jnp.int32, (EXTRA, nloc), 0)

    def block(q, g0, ng):
        pair = jnp.concatenate([bs[2 * q, 0:naux, :], bs[2 * q + 1, 0:naux, :]], axis=1)
        a = gt[g0 : g0 + ng].reshape(ng * nloc, naux)
        work[0 : ng * nloc, :] = jnp.dot(a, pair, preferred_element_type=F32)
        mine = bs[own, naux : naux + EXTRA, :].astype(F32)
        for k in range(2):
            j_off = jnp.where(q == 5, 6 - 11 * k, 2 * (q - 2) + k)
            e_sum = e_own + occ[omap[around(2 * chip - wide + j_off)]]
            delta = core - j_off
            theirs = bs[2 * q + k, naux : naux + EXTRA, :].astype(F32)
            pick = jnp.where(delta >= 0, mine, theirs)
            w = jnp.sum(jnp.where(rows16 == jnp.abs(delta), pick, 0.0), axis=0, keepdims=True)
            for g in range(g0, g0 + ng):
                v = work[(g - g0) * nloc : (g - g0 + 1) * nloc, k * nloc : (k + 1) * nloc]
                t = w * v / ((va[g] + vb) - e_sum)
                tt[pl.ds((2 * q + k) * nloc, nloc), COLUMN[g] * nloc : (COLUMN[g] + 1) * nloc] = t.T.astype(BF16)

    def pair_at(i):
        q = 0
        for x in range(NX):
            for j, value in enumerate(ORDER[x]):
                q = jnp.where(jnp.logical_and(cx == x, i == j), value, q)
        return q

    def blocks(first, last, g0, ng, wait=False):
        @pl.loop(first, last)
        def _(i):
            q = pair_at(i)
            if wait:
                shared(2 * q + 1 - core)
            block(q, g0, ng)

    run(1)
    blocks(0, 3, 0, 3, True)
    run(2)
    blocks(0, 3, 3, 2)
    blocks(3, 4, 0, 5, True)
    run(3)
    blocks(4, 5, 0, 5, True)
    run(4)
    blocks(0, 5, 5, 2)
    run(5)
    blocks(5, 6, 0, 7, True)
    run(6)
    run(7)
    blocks(0, 6, 7, 1)

    quarter = naux // 4

    def rows_of(part):
        return pl.ds(pl.multiple_of(part * quarter, quarter), quarter)

    def tile(p, part):
        lhs = jnp.concatenate([bs[s, rows_of(part), :] for s in range(SLOTS)], axis=1)
        cols = pl.ds(pl.multiple_of(p * 2 * nloc, 2 * nloc), 2 * nloc)
        work[0:quarter, :] = jnp.dot(lhs, tt[:, cols], preferred_element_type=F32)

    def beside(way):
        return (wide, jnp.where(way == 0, right[1], left[1]))

    def y_copy(i, way):
        return remote(sy.at[i], ry.at[i], sy_sem.at[i], ry_sem.at[i], beside(way))

    def n_copy(i, device):
        return remote(sn.at[i], rn.at[i], sn_sem.at[i], rn_sem.at[i], device)

    def took_y(i):
        arrived(ry.at[i], ry_sem.at[i])
        return decode(ry.at[i], quarter)

    def took_n(i):
        arrived(rn.at[i], rn_sem.at[i])
        return decode(rn.at[i], quarter)

    def y_step(stage):
        @pl.loop(0, 2)
        def _(way):
            tile(3 if stage == 0 else 1 + way, 1 - way if stage == 1 else way)
            value = work[0:quarter, :]
            if stage == 2:
                value = value + took_y(way)
            encode(value, sy.at[2 * stage + way])
            y_copy(2 * stage + way, way).start()

    def z_step(p):
        @pl.loop(0, 2)
        def _(j):
            tile(p, 2 + j)
            keep[2 * p + j] = work[0:quarter, 0:nloc]
            encode(work[0:quarter, nloc : 2 * nloc], sn.at[2 * p + j])
            n_copy(2 * p + j, zpart).start()

    def n_step(stage):
        @pl.loop(0, 2)
        def _(way):
            i = 6 + way if stage == 0 else 2 * (1 + way) + (1 - way if stage == 1 else way)
            value = keep[i] + took_n(i)
            if stage == 2:
                value = value + took_n(8 + way)
            encode(value, sn.at[8 + 2 * stage + way])
            n_copy(8 + 2 * stage + way, beside(way)).start()

    y_step(0)
    z_step(3)
    y_step(1)
    z_step(1)
    y_step(2)
    z_step(2)
    n_step(0)
    z_step(0)
    n_step(1)

    @pl.loop(0, 2)
    def _(part):
        tile(0, part)
        total = work[0:quarter, :] + took_y(4 - 2 * part) + took_y(3 + 2 * part)
        out[rows_of(part), :] = total[:, 0:nloc]
        encode(total[:, nloc : 2 * nloc], sn.at[14 + part])
        n_copy(14 + part, zpart).start()

    n_step(2)

    @pl.loop(0, 2)
    def _(j):
        out[rows_of(2 + j), :] = keep[j] + took_n(j) + took_n(12 - 2 * j) + took_n(11 + 2 * j)

    @pl.loop(0, 2)
    def _(part):
        out[rows_of(part), :] += took_n(14 + part)

    run(0, True)

    @pl.loop(0, 6)
    def _(i):
        y_copy(i, i % 2).wait_send()

    @pl.loop(0, 16)
    def _(i):
        n_copy(i, sib).wait_send()


def per_device(three_index, orbital_map, occ_energy, vir_energy, pair_kept):
    _, naux, nloc = three_index.shape
    n_wide = lax.axis_size("wide")
    n_narrow = lax.axis_size("narrow")
    x = three_index.reshape(naux, nloc)
    kept = jnp.pad(pair_kept, ((0, EXTRA - pair_kept.shape[0]), (0, 0))).astype(BF16)
    kept = jnp.broadcast_to(kept, (EXTRA, nloc))
    vir = vir_energy.reshape(n_narrow, nloc)
    quarter = naux // 4
    vmem = functools.partial(pl.BlockSpec, memory_space=pltpu.VMEM)
    smem = functools.partial(pl.BlockSpec, memory_space=pltpu.SMEM)
    hbm = functools.partial(pl.BlockSpec, memory_space=pl.ANY)
    dma = pltpu.SemaphoreType.DMA
    density = pl.pallas_call(
        functools.partial(kernel, n_wide, naux, nloc),
        out_shape=jax.ShapeDtypeStruct((naux, nloc), F32),
        in_specs=[smem(), smem(), hbm(), hbm(), hbm(), vmem()],
        out_specs=vmem(),
        scratch_shapes=[
            pltpu.VMEM((SLOTS + RELAYS, naux + EXTRA, nloc), BF16),
            pltpu.VMEM((8, nloc, naux), BF16),
            pltpu.VMEM((8, nloc, nloc), F32),
            pltpu.VMEM((SLOTS * nloc, 8 * nloc), BF16),
            pltpu.VMEM((8 * nloc, 2 * nloc), F32),
            pltpu.VMEM((8, quarter, nloc), F32),
            pltpu.VMEM((6, quarter + EXTRA, 2 * nloc), jnp.int16),
            pltpu.VMEM((6, quarter + EXTRA, 2 * nloc), jnp.int16),
            pltpu.VMEM((16, quarter + EXTRA, nloc), jnp.int16),
            pltpu.VMEM((16, quarter + EXTRA, nloc), jnp.int16),
            dma((3,)),
            dma((32,)),
            dma((SLOTS + RELAYS, 2)),
            dma((6,)),
            dma((SLOTS,)),
            dma((8, 2)),
            dma((6,)),
            dma((6,)),
            dma((16,)),
            dma((16,)),
        ],
        compiler_params=pltpu.CompilerParams(
            collective_id=0, has_side_effects=True, vmem_limit_bytes=60 * 1024 * 1024
        ),
    )(orbital_map, occ_energy, x, x.T, kept, vir)
    return density.reshape(1, naux, nloc)


def solution(mesh):
    placed = (P("wide", None, "narrow"), P(), P(), P(), P(None, "wide"))
    return jax.shard_map(
        per_device, mesh=mesh, in_specs=placed, out_specs=P("wide", None, "narrow"), check_vma=False
    )
```

```python
import collections
import functools
import heapq

import jax
import jax.numpy as jnp
from jax import lax
from jax.experimental import pallas as pl
from jax.experimental.pallas import tpu as pltpu
from jax.sharding import PartitionSpec as P

MESH = pl.DeviceIdType.MESH
F32 = jnp.float32
BF16 = jnp.bfloat16

NX, NY, NZL = 4, 4, 2
EXTRA = 16
SLOTS = 12
LN2 = 0.6931471805599453
FINE = 64.0
TOP = 32000.0
COLUMN = (0, 2, 4, 6, 1, 3, 5, 7)

HOP = 0.2
ROUTES = {
    (3, 1): ((3, ((3, 0), (0, 1), (3, 2))),),
    (3, 0): ((0, ((0, 1),)),),
    (2, 1): ((1, ((1, 0),)),),
    (2, 0): ((2, ((2, 1), (1, 0))),),
    (1, 1): ((1, ((1, 0),)), (0, ())),
}
ORDER = ((2, 3, 4, 5, 1, 0), (1, 2, 3, 4, 5, 0), (1, 2, 3, 0, 5, 4), (0, 1, 2, 5, 3, 4))
PHASES = ((3, 3), (4, 5), (5, 5), (5, 7), (6, 7), (6, 8))
RELAYS = 2


def slot_of(x, k, dz, owner):
    off = NX * dz + owner - x
    if -2 <= off <= 2:
        return 2 * (off + 2) + k
    if off == 3 and k == 0:
        return 10
    if off == -3 and k == 1:
        return 11
    return None


def messages():
    out = []

    def fw(k, xs, xd, dz, owner, h, rank=1):
        xs, xd, owner = xs % NX, xd % NX, owner % NX
        kind = "x+" if (xs + 1) % NX == xd else "x-"
        out.append((("S", dz, owner, h), kind, xs, xd, k, ("S", dz, owner, h), rank))

    for k in (0, 1):
        for x in range(NX):
            for h in (0, 1):
                fw(k, x, x + 1, 0, x, h, 2 + 0.1 * h)
                fw(k, x, x - 1, 0, x, 1 - h, 2 + 0.1 * h)
            fw(k, x + 1, x + 2, 0, x, 0)
            fw(k, x - 1, x - 2, 0, x, 1)
        for up in (True, False):
            kk, dz = (k, -1) if up else (1 - k, 1)

            def m(v, up=up):
                return v if up else NX - 1 - v

            for (owner, odd), ways in ROUTES.items():
                for h in (0, 1) if odd == k else ():
                    column, edges = ways[h * len(ways) // 2]
                    g = h if up else 1 - h
                    sent, got = ("S", 0, m(owner), g), ("S", dz, m(owner), g)
                    out.append((sent, "z+" if up else "z-", m(column), m(column), kk, got, 1))
                    for xs, xd in edges:
                        fw(kk, m(xs), m(xd), dz, m(owner), g, 0)
        for x in range(NX):

            def ag(g0, kind, g1, h, rank, k=k, x=x):
                out.append((("A", g0, h), kind, x, x, k, ("A", g1, h), rank))

            for h in (0, 1):
                ag(0, "zz", 4, h, 1 + 0.1 * h)
                ag(0, "y+", 2, h, 2 + 0.1 * h)
                ag(0, "y-", 1, 1 - h, 2 + 0.1 * h)
                ag(4, "y+", 6, h, 3)
                ag(4, "y-", 5, 1 - h, 3)
            ag(2, "y+", 3, 0, 1)
            ag(1, "y-", 3, 1, 1)
            ag(6, "y+", 7, 0, 1)
            ag(5, "y-", 7, 1, 1)
    return out


@functools.cache
def programs():
    ms = messages()
    devices = [(x, k) for x in range(NX) for k in (0, 1)]
    need, queues, flying, have, ready, clock = {}, {}, {}, {}, {}, 0.0
    for i, m in enumerate(ms):
        need.setdefault((m[2], m[4], m[0]), []).append(i)
    ops = {device: [(0.0, 9, 0, "share", 4 + device[1])] for device in devices}
    coming = [(0.0, x, k, z, item) for x, k in devices for z in (0, 1) for h in (0, 1)
              for item in (("S", 0, x, h), ("A", 0, h))]
    heapq.heapify(coming)
    while coming or flying:
        while coming and coming[0][0] <= clock + 1e-9:
            t, x, k, z, item = heapq.heappop(coming)
            have[x, k, item] = max(have.get((x, k, item), 0.0), t)
            for i in need.get((x, k, item), ()):
                kind = ("z-" if z else "z+") if ms[i][1] == "zz" else ms[i][1]
                heapq.heappush(queues.setdefault((kind, x, k, z), []), (t, ms[i][6], i, z))
                ready[i] = max(ready.get(i, 0.0), t)
        for key, queue in queues.items():
            if queue and key not in flying:
                _, _, i, z = heapq.heappop(queue)
                _, kind, x, *_ = ms[i]
                if kind == "zz":
                    links = [("even", "z-" if z else "z+", x)]
                elif kind in ("z+", "z-"):
                    links = [("even", kind, x), ("odd", kind, x)]
                else:
                    links = [(kind, x, z)]
                flying[key] = [i, z, 0.5, links]
        users = collections.Counter(link for flight in flying.values() for link in flight[3])
        rate = {key: min(1.0 / users[link] for link in flight[3]) for key, flight in flying.items()}
        step = min([flight[2] / rate[key] for key, flight in flying.items()], default=1e9)
        if coming:
            step = min(step, max(coming[0][0] - clock, 0.0))
        clock += step
        for key, flight in list(flying.items()):
            flight[2] -= rate[key] * step
            if flight[2] <= 1e-7:
                i, z, _, links = flying.pop(key)
                _, kind, _, xd, k, item, _ = ms[i]
                heapq.heappush(coming, (clock + HOP * len(links), xd, k, 1 - z if kind == "zz" else z, item))
    for i, (item, kind, xs, xd, k, item2, rank) in enumerate(ms):
        ops[xs, k].append((ready[i], rank, i, "send", item, kind, xd, item2))
        ops[xd, k].append((have[xd, k, item2], -1, i, "wait", item2))
    for (x, k), program in ops.items():
        for dz in (-1, 0, 1):
            for owner in range(NX):
                both = [have.get((x, k, ("S", dz, owner, h))) for h in (0, 1)]
                slot = slot_of(x, k, dz, owner)
                if slot is not None and slot != 4 + k:
                    program.append((max(both), 1, 0, "share", slot))
        program.sort(key=lambda op: op[:3])
    return ops


@functools.cache
def phase_ends(x, k):
    ends, end = [], 0.01
    for pairs, slices in PHASES:
        slots = [2 * q + c for q in ORDER[x][:pairs] for c in (0, 1)]
        for core in (0, 1):
            for op in programs()[x, core]:
                if op[3] == "share" and op[4] in slots:
                    end = max(end, op[0])
                if op[3] == "wait" and op[4][0] == "A" and core == k and op[4][1] < slices:
                    end = max(end, op[0])
        ends.append(end)
    return [0.01, *ends, 1000.0]


def places(x, k):
    found, spare = {}, SLOTS
    for op in programs()[x, k]:
        if op[3] == "wait" and op[4][0] == "S" and op[4][:3] not in found:
            slot = slot_of(x, k, op[4][1], op[4][2])
            if slot is None:
                slot, spare = spare, spare + 1
            found[op[4][:3]] = slot
    found["S", 0, x] = 4 + k
    assert spare <= SLOTS + RELAYS
    return found


def scale_of(level):
    return jnp.exp(level * (LN2 / FINE))


def encode(value, ref):
    rows = value.shape[0]
    top = jnp.maximum(jnp.max(jnp.abs(value), axis=0, keepdims=True), 1e-25)
    level = jnp.ceil(jnp.log(top) * (FINE / LN2))
    factor = TOP / scale_of(level)
    ref[0:rows, :] = jnp.round(value * factor).astype(jnp.int32).astype(jnp.int16)
    spread = jnp.broadcast_to(level, (EXTRA, value.shape[1]))
    ref[rows : rows + EXTRA, :] = spread.astype(jnp.int32).astype(jnp.int16)


def decode(ref, rows):
    level = ref[rows : rows + EXTRA, :].astype(jnp.int32).astype(F32)[0:1, :]
    return ref[0:rows, :].astype(jnp.int32).astype(F32) * (scale_of(level) * (1.0 / TOP))


def kernel(n_wide, naux, nloc, rounds, omap, occ, kept, x, vir, out, bs, gt, va, tt, work, keep, sy, ry, sn, rn,
           loc_sem, w_send, w_recv, s_send, s_recv, g_recv, sy_sem, ry_sem, sn_sem, rn_sem):
    wide = lax.axis_index("wide")
    narrow = lax.axis_index("narrow")
    core = wide % 2
    chip = wide // 2
    cx = chip % NX
    zh8 = wide - wide % (2 * NX)
    zl, cy = narrow // NY, narrow % NY

    def around(by):
        return (wide + by + n_wide) % n_wide

    def ringx(by):
        return zh8 + ((cx + by + NX) % NX) * 2 + core

    sib = (wide + 1 - 2 * core, narrow)
    right = (wide, zl * NY + (cy + 1) % NY)
    left = (wide, zl * NY + (cy + NY - 1) % NY)
    zpart = (wide, (1 - zl) * NY + cy)
    zup, zdown = (around(2 * NX), narrow), (around(-2 * NX), narrow)
    xup, xdown = (ringx(1), narrow), (ringx(-1), narrow)
    to = {"x+": xup, "x-": xdown, "z+": zup, "z-": zdown, "zz": zpart, "y+": right, "y-": left}

    half = naux // 2
    halves = (pl.ds(0, half), pl.ds(half, half + EXTRA))
    lo_hi = (pl.ds(0, nloc // 2), pl.ds(nloc // 2, nloc // 2))
    own = 4 + core

    local = [
        pltpu.make_async_copy(x, bs.at[own, pl.ds(0, naux)], loc_sem.at[0]),
    ]
    for c in local:
        c.start()
    barrier = pltpu.get_barrier_semaphore()
    greeted = [sib, *to.values()]
    for device in greeted:
        pl.semaphore_signal(barrier, inc=1, device_id=device, device_id_type=MESH)
    rows16 = lax.broadcasted_iota(jnp.int32, (EXTRA, nloc), 0)
    weights = jnp.zeros((EXTRA, nloc), F32)
    for r in range(rounds):
        weights = jnp.where(rows16 == r, kept[r].astype(F32), weights)
    bs[own, naux : naux + EXTRA, :] = weights.astype(BF16)
    for c in local:
        c.wait()
    for r in range(0, naux, nloc):
        gt[0, :, r : r + nloc] = bs[own, r : r + nloc, :].T
    pl.semaphore_wait(barrier, len(greeted))

    def remote(src, dst, s_sem, r_sem, device):
        return pltpu.make_async_remote_copy(src_ref=src, dst_ref=dst, send_sem=s_sem, recv_sem=r_sem,
                                            device_id=device, device_id_type=MESH)

    def arrived(dst, r_sem):
        remote(dst, dst, w_send.at[0], r_sem, sib).wait_recv()

    def view(item, place):
        if item[0] == "S":
            slot, h = place[item[:3]], item[3]
            return bs.at[slot, halves[h]], w_recv.at[slot, h]
        return gt.at[item[1], lo_hi[item[2]]], g_recv.at[item[1], item[2]]

    def run(phase, finish=False):
        for x in range(NX):
            for k in (0, 1):

                @pl.when(jnp.logical_and(cx == x, core == k))
                def _(x=x, k=k):
                    place, n_sent, n_shared = places(x, k), 0, 0
                    ends = [-1.0, *phase_ends(x, k)]
                    for op in programs()[x, k]:
                        now = not finish and ends[phase] < op[0] <= ends[phase + 1]
                        if op[3] == "wait":
                            if now:
                                arrived(*view(op[4], place))
                        elif op[3] == "share":
                            part = bs.at[op[4]]
                            if now:
                                remote(part, part, s_send.at[n_shared], s_recv.at[op[4]], sib).start()
                            if finish:
                                remote(part, part, s_send.at[n_shared], s_recv.at[op[4]], sib).wait_send()
                            n_shared += 1
                        else:
                            _, _, _, _, item, kind, xd, there = op
                            dst, r_sem = view(there, places(xd, k))
                            if now:
                                remote(view(item, place)[0], dst, w_send.at[n_sent], r_sem, to[kind]).start()
                            if finish:
                                remote(view(item, place)[0], dst, w_send.at[n_sent], r_sem, to[kind]).wait_send()
                            n_sent += 1

    def shared(slot):
        arrived(bs.at[slot], s_recv.at[slot])

    run(0)

    gy = (0, 1, 3, 2) * 2
    gz = (0,) * 4 + (1,) * 4
    for g in range(8):
        row = vir[pl.ds(((zl + gz[g]) % NZL) * NY + (cy + gy[g]) % NY, 1), :]
        va[g] = jnp.broadcast_to(row, (nloc, nloc)).T
    vb = vir[pl.ds(narrow, 1), :]
    e_own = occ[omap[wide]]

    def block(q, g0, ng):
        pair = jnp.concatenate([bs[2 * q, 0:naux, :], bs[2 * q + 1, 0:naux, :]], axis=1)
        a = gt[g0 : g0 + ng].reshape(ng * nloc, naux)
        work[0 : ng * nloc, :] = jnp.dot(a, pair, preferred_element_type=F32)
        mine = bs[own, naux : naux + EXTRA, :].astype(F32)
        for k in range(2):
            j_off = jnp.where(q == 5, 6 - 11 * k, 2 * (q - 2) + k)
            e_sum = e_own + occ[omap[around(2 * chip - wide + j_off)]]
            delta = core - j_off
            theirs = bs[2 * q + k, naux : naux + EXTRA, :].astype(F32)
            pick = jnp.where(delta >= 0, mine, theirs)
            w = jnp.sum(jnp.where(rows16 == jnp.abs(delta), pick, 0.0), axis=0, keepdims=True)
            for g in range(g0, g0 + ng):
                v = work[(g - g0) * nloc : (g - g0 + 1) * nloc, k * nloc : (k + 1) * nloc]
                t = w * v / ((va[g] + vb) - e_sum)
                tt[pl.ds((2 * q + k) * nloc, nloc), COLUMN[g] * nloc : (COLUMN[g] + 1) * nloc] = t.T.astype(BF16)

    def pair_at(i):
        q = 0
        for x in range(NX):
            for j, value in enumerate(ORDER[x]):
                q = jnp.where(jnp.logical_and(cx == x, i == j), value, q)
        return q

    def blocks(first, last, g0, ng, wait=False):
        @pl.loop(first, last)
        def _(i):
            q = pair_at(i)
            if wait:
                shared(2 * q + 1 - core)
            block(q, g0, ng)

    run(1)
    blocks(0, 3, 0, 3, True)
    run(2)
    blocks(0, 3, 3, 2)
    blocks(3, 4, 0, 5, True)
    run(3)
    blocks(4, 5, 0, 5, True)
    run(4)
    blocks(0, 5, 5, 2)
    run(5)
    blocks(5, 6, 0, 7, True)
    quarter = naux // 4

    def rows_of(part):
        return pl.ds(pl.multiple_of(part * quarter, quarter), quarter)

    def tile(p, part):
        lhs = jnp.concatenate([bs[s, rows_of(part), :] for s in range(SLOTS)], axis=1)
        cols = pl.ds(pl.multiple_of(p * 2 * nloc, 2 * nloc), 2 * nloc)
        work[0:quarter, :] = jnp.dot(lhs, tt[:, cols], preferred_element_type=F32)

    def beside(way):
        return (wide, jnp.where(way == 0, right[1], left[1]))

    def y_copy(i, way):
        return remote(sy.at[i], ry.at[i], sy_sem.at[i], ry_sem.at[i], beside(way))

    def n_copy(i, device):
        return remote(sn.at[i], rn.at[i], sn_sem.at[i], rn_sem.at[i], device)

    def took_y(i):
        arrived(ry.at[i], ry_sem.at[i])
        return decode(ry.at[i], quarter)

    def took_n(i):
        arrived(rn.at[i], rn_sem.at[i])
        return decode(rn.at[i], quarter)

    def y_step(stage):
        @pl.loop(0, 2)
        def _(way):
            tile(3 if stage == 0 else 1 + way, 1 - way if stage == 1 else way)
            value = work[0:quarter, :]
            if stage == 2:
                value = value + took_y(way)
            encode(value, sy.at[2 * stage + way])
            y_copy(2 * stage + way, way).start()

    def z_step(p):
        @pl.loop(0, 2)
        def _(j):
            tile(p, 2 + j)
            keep[2 * p + j] = work[0:quarter, 0:nloc]
            encode(work[0:quarter, nloc : 2 * nloc], sn.at[2 * p + j])
            n_copy(2 * p + j, zpart).start()

    def n_step(stage):
        @pl.loop(0, 2)
        def _(way):
            i = 6 + way if stage == 0 else 2 * (1 + way) + (1 - way if stage == 1 else way)
            value = keep[i] + took_n(i)
            if stage == 2:
                value = value + took_n(8 + way)
            encode(value, sn.at[8 + 2 * stage + way])
            n_copy(8 + 2 * stage + way, beside(way)).start()

    y_step(1)
    z_step(1)
    run(6)
    run(7)
    blocks(0, 6, 7, 1)
    y_step(0)
    z_step(3)
    z_step(2)
    y_step(2)
    n_step(0)
    z_step(0)
    n_step(1)

    @pl.loop(0, 2)
    def _(part):
        tile(0, part)
        total = work[0:quarter, :] + took_y(4 - 2 * part) + took_y(3 + 2 * part)
        out[rows_of(part), :] = total[:, 0:nloc]
        encode(total[:, nloc : 2 * nloc], sn.at[14 + part])
        n_copy(14 + part, zpart).start()

    n_step(2)

    @pl.loop(0, 2)
    def _(j):
        out[rows_of(2 + j), :] = keep[j] + took_n(j) + took_n(12 - 2 * j) + took_n(11 + 2 * j)

    @pl.loop(0, 2)
    def _(part):
        out[rows_of(part), :] += took_n(14 + part)

    run(0, True)

    @pl.loop(0, 6)
    def _(i):
        y_copy(i, i % 2).wait_send()

    @pl.loop(0, 16)
    def _(i):
        n_copy(i, sib).wait_send()


def per_device(three_index, orbital_map, occ_energy, vir_energy, pair_kept):
    _, naux, nloc = three_index.shape
    n_wide = lax.axis_size("wide")
    n_narrow = lax.axis_size("narrow")
    x = three_index.reshape(naux, nloc)
    kept = pair_kept.reshape(-1)
    vir = vir_energy.reshape(n_narrow, nloc)
    quarter = naux // 4
    vmem = functools.partial(pl.BlockSpec, memory_space=pltpu.VMEM)
    smem = functools.partial(pl.BlockSpec, memory_space=pltpu.SMEM)
    hbm = functools.partial(pl.BlockSpec, memory_space=pl.ANY)
    dma = pltpu.SemaphoreType.DMA
    density = pl.pallas_call(
        functools.partial(kernel, n_wide, naux, nloc, kept.shape[0]),
        out_shape=jax.ShapeDtypeStruct((naux, nloc), F32),
        in_specs=[smem(), smem(), smem(), hbm(), vmem()],
        out_specs=vmem(),
        scratch_shapes=[
            pltpu.VMEM((SLOTS + RELAYS, naux + EXTRA, nloc), BF16),
            pltpu.VMEM((8, nloc, naux), BF16),
            pltpu.VMEM((8, nloc, nloc), F32),
            pltpu.VMEM((SLOTS * nloc, 8 * nloc), BF16),
            pltpu.VMEM((8 * nloc, 2 * nloc), F32),
            pltpu.VMEM((8, quarter, nloc), F32),
            pltpu.VMEM((6, quarter + EXTRA, 2 * nloc), jnp.int16),
            pltpu.VMEM((6, quarter + EXTRA, 2 * nloc), jnp.int16),
            pltpu.VMEM((16, quarter + EXTRA, nloc), jnp.int16),
            pltpu.VMEM((16, quarter + EXTRA, nloc), jnp.int16),
            dma((1,)),
            dma((32,)),
            dma((SLOTS + RELAYS, 2)),
            dma((6,)),
            dma((SLOTS,)),
            dma((8, 2)),
            dma((6,)),
            dma((6,)),
            dma((16,)),
            dma((16,)),
        ],
        compiler_params=pltpu.CompilerParams(
            collective_id=0, has_side_effects=True, vmem_limit_bytes=60 * 1024 * 1024
        ),
    )(orbital_map, occ_energy, kept, x, vir)
    return density.reshape(1, naux, nloc)


def solution(mesh):
    placed = (P("wide", None, "narrow"), P(), P(), P(), P(None, "wide"))
    return jax.shard_map(
        per_device, mesh=mesh, in_specs=placed, out_specs=P("wide", None, "narrow"), check_vma=False
    )
```

```python
import collections
import functools
import heapq

import jax
import jax.numpy as jnp
from jax import lax
from jax.experimental import pallas as pl
from jax.experimental.pallas import tpu as pltpu
from jax.sharding import PartitionSpec as P

MESH = pl.DeviceIdType.MESH
F32 = jnp.float32
BF16 = jnp.bfloat16

NX, NY, NZL = 4, 4, 2
EXTRA = 16
Y_ROWS = 832
SLOTS = 12
LN2 = 0.6931471805599453
FINE = 64.0
TOP = 32000.0
COLUMN = (0, 2, 4, 6, 1, 3, 5, 7)

HOP = 0.2
ROUTES = {
    (3, 1): ((3, ((3, 0), (0, 1), (3, 2))),),
    (3, 0): ((0, ((0, 1),)),),
    (2, 1): ((1, ((1, 0),)),),
    (2, 0): ((2, ((2, 1), (1, 0))),),
    (1, 1): ((1, ((1, 0),)), (0, ())),
}
ORDER = ((2, 3, 4, 5, 1, 0), (1, 2, 3, 4, 5, 0), (1, 2, 3, 0, 5, 4), (0, 1, 2, 5, 3, 4))
PHASES = ((3, 3), (4, 5), (5, 5), (5, 7), (6, 7), (6, 8))
RELAYS = 2


def slot_of(x, k, dz, owner):
    off = NX * dz + owner - x
    if -2 <= off <= 2:
        return 2 * (off + 2) + k
    if off == 3 and k == 0:
        return 10
    if off == -3 and k == 1:
        return 11
    return None


def messages():
    out = []

    def fw(k, xs, xd, dz, owner, h, rank=1):
        xs, xd, owner = xs % NX, xd % NX, owner % NX
        kind = "x+" if (xs + 1) % NX == xd else "x-"
        out.append((("S", dz, owner, h), kind, xs, xd, k, ("S", dz, owner, h), rank))

    for k in (0, 1):
        for x in range(NX):
            for h in (0, 1):
                fw(k, x, x + 1, 0, x, h, 2 + 0.1 * h)
                fw(k, x, x - 1, 0, x, 1 - h, 2 + 0.1 * h)
            fw(k, x + 1, x + 2, 0, x, 0)
            fw(k, x - 1, x - 2, 0, x, 1)
        for up in (True, False):
            kk, dz = (k, -1) if up else (1 - k, 1)

            def m(v, up=up):
                return v if up else NX - 1 - v

            for (owner, odd), ways in ROUTES.items():
                for h in (0, 1) if odd == k else ():
                    column, edges = ways[h * len(ways) // 2]
                    g = h if up else 1 - h
                    sent, got = ("S", 0, m(owner), g), ("S", dz, m(owner), g)
                    out.append((sent, "z+" if up else "z-", m(column), m(column), kk, got, 1))
                    for xs, xd in edges:
                        fw(kk, m(xs), m(xd), dz, m(owner), g, 0)
        for x in range(NX):

            def ag(g0, kind, g1, h, rank, k=k, x=x):
                out.append((("A", g0, h), kind, x, x, k, ("A", g1, h), rank))

            for h in (0, 1):
                ag(0, "zz", 4, h, 3 + 0.1 * h)
                ag(0, "y+", 2, h, 2 + 0.1 * h)
                ag(0, "y-", 1, 1 - h, 2 + 0.1 * h)
                ag(4, "y+", 6, h, 3)
                ag(4, "y-", 5, 1 - h, 3)
            ag(2, "y+", 3, 0, 1)
            ag(1, "y-", 3, 1, 1)
            ag(6, "y+", 7, 0, 1)
            ag(5, "y-", 7, 1, 1)
    return out


@functools.cache
def programs():
    ms = messages()
    devices = [(x, k) for x in range(NX) for k in (0, 1)]
    need, queues, flying, have, ready, clock = {}, {}, {}, {}, {}, 0.0
    for i, m in enumerate(ms):
        need.setdefault((m[2], m[4], m[0]), []).append(i)
    ops = {device: [(0.0, 9, 0, "share", 4 + device[1])] for device in devices}
    coming = [(0.0, x, k, z, item) for x, k in devices for z in (0, 1) for h in (0, 1)
              for item in (("S", 0, x, h), ("A", 0, h))]
    heapq.heapify(coming)
    while coming or flying:
        while coming and coming[0][0] <= clock + 1e-9:
            t, x, k, z, item = heapq.heappop(coming)
            have[x, k, item] = max(have.get((x, k, item), 0.0), t)
            for i in need.get((x, k, item), ()):
                kind = ("z-" if z else "z+") if ms[i][1] == "zz" else ms[i][1]
                heapq.heappush(queues.setdefault((kind, x, k, z), []), (t, ms[i][6], i, z))
                ready[i] = max(ready.get(i, 0.0), t)
        for key, queue in queues.items():
            if queue and key not in flying:
                _, _, i, z = heapq.heappop(queue)
                _, kind, x, *_ = ms[i]
                if kind == "zz":
                    links = [("even", "z-" if z else "z+", x)]
                elif kind in ("z+", "z-"):
                    links = [("even", kind, x), ("odd", kind, x)]
                else:
                    links = [(kind, x, z)]
                flying[key] = [i, z, 0.5, links]
        users = collections.Counter(link for flight in flying.values() for link in flight[3])
        rate = {key: min(1.0 / users[link] for link in flight[3]) for key, flight in flying.items()}
        step = min([flight[2] / rate[key] for key, flight in flying.items()], default=1e9)
        if coming:
            step = min(step, max(coming[0][0] - clock, 0.0))
        clock += step
        for key, flight in list(flying.items()):
            flight[2] -= rate[key] * step
            if flight[2] <= 1e-7:
                i, z, _, links = flying.pop(key)
                _, kind, _, xd, k, item, _ = ms[i]
                heapq.heappush(coming, (clock + HOP * len(links), xd, k, 1 - z if kind == "zz" else z, item))
    for i, (item, kind, xs, xd, k, item2, rank) in enumerate(ms):
        ops[xs, k].append((ready[i], rank, i, "send", item, kind, xd, item2))
        ops[xd, k].append((have[xd, k, item2], -1, i, "wait", item2))
    for (x, k), program in ops.items():
        for dz in (-1, 0, 1):
            for owner in range(NX):
                both = [have.get((x, k, ("S", dz, owner, h))) for h in (0, 1)]
                slot = slot_of(x, k, dz, owner)
                if slot is not None and slot != 4 + k:
                    program.append((max(both), 1, 0, "share", slot))
        program.sort(key=lambda op: op[:3])
    return ops


@functools.cache
def phase_ends(x, k):
    ends, end = [], 0.01
    for pairs, slices in PHASES:
        slots = [2 * q + c for q in ORDER[x][:pairs] for c in (0, 1)]
        for core in (0, 1):
            for op in programs()[x, core]:
                if op[3] == "share" and op[4] in slots:
                    end = max(end, op[0])
                if op[3] == "wait" and op[4][0] == "A" and core == k and op[4][1] < slices:
                    end = max(end, op[0])
        ends.append(end)
    return [0.01, *ends, 1000.0]


def places(x, k):
    found, spare = {}, SLOTS
    for op in programs()[x, k]:
        if op[3] == "wait" and op[4][0] == "S" and op[4][:3] not in found:
            slot = slot_of(x, k, op[4][1], op[4][2])
            if slot is None:
                slot, spare = spare, spare + 1
            found[op[4][:3]] = slot
    found["S", 0, x] = 4 + k
    assert spare <= SLOTS + RELAYS
    return found


def scale_of(level):
    return jnp.exp(level * (LN2 / FINE))


def encode(value, ref):
    rows = value.shape[0]
    top = jnp.maximum(jnp.max(jnp.abs(value), axis=0, keepdims=True), 1e-25)
    level = jnp.ceil(jnp.log(top) * (FINE / LN2))
    factor = TOP / scale_of(level)
    ref[0:rows, :] = jnp.round(value * factor).astype(jnp.int32).astype(jnp.int16)
    spread = jnp.broadcast_to(level, (EXTRA, value.shape[1]))
    ref[rows : rows + EXTRA, :] = spread.astype(jnp.int32).astype(jnp.int16)


def decode(ref, rows):
    level = ref[rows : rows + EXTRA, :].astype(jnp.int32).astype(F32)[0:1, :]
    return ref[0:rows, :].astype(jnp.int32).astype(F32) * (scale_of(level) * (1.0 / TOP))


def kernel(n_wide, naux, nloc, rounds, omap, occ, kept, x, vir, out, bs, gt, va, tt, work, keep, sy, ry, sn, rn,
           loc_sem, w_send, w_recv, s_send, s_recv, g_recv, sy_sem, ry_sem, sn_sem, rn_sem):
    wide = lax.axis_index("wide")
    narrow = lax.axis_index("narrow")
    core = wide % 2
    chip = wide // 2
    cx = chip % NX
    zh8 = wide - wide % (2 * NX)
    zl, cy = narrow // NY, narrow % NY

    def around(by):
        return (wide + by + n_wide) % n_wide

    def ringx(by):
        return zh8 + ((cx + by + NX) % NX) * 2 + core

    sib = (wide + 1 - 2 * core, narrow)
    right = (wide, zl * NY + (cy + 1) % NY)
    left = (wide, zl * NY + (cy + NY - 1) % NY)
    zpart = (wide, (1 - zl) * NY + cy)
    zup, zdown = (around(2 * NX), narrow), (around(-2 * NX), narrow)
    xup, xdown = (ringx(1), narrow), (ringx(-1), narrow)
    to = {"x+": xup, "x-": xdown, "z+": zup, "z-": zdown, "zz": zpart, "y+": right, "y-": left}

    half = naux // 2
    halves = (pl.ds(0, half), pl.ds(half, half + EXTRA))
    lo_hi = (pl.ds(0, nloc // 2), pl.ds(nloc // 2, nloc // 2))
    own = 4 + core

    local = [
        pltpu.make_async_copy(x, bs.at[own, pl.ds(0, naux)], loc_sem.at[0]),
    ]
    for c in local:
        c.start()
    barrier = pltpu.get_barrier_semaphore()
    greeted = [sib, *to.values()]
    for device in greeted:
        pl.semaphore_signal(barrier, inc=1, device_id=device, device_id_type=MESH)
    rows16 = lax.broadcasted_iota(jnp.int32, (EXTRA, nloc), 0)
    weights = jnp.zeros((EXTRA, nloc), F32)
    for r in range(rounds):
        weights = jnp.where(rows16 == r, kept[r].astype(F32), weights)
    bs[own, naux : naux + EXTRA, :] = weights.astype(BF16)
    for c in local:
        c.wait()
    for r in range(0, naux, nloc):
        gt[0, :, r : r + nloc] = bs[own, r : r + nloc, :].T
    pl.semaphore_wait(barrier, len(greeted))

    def remote(src, dst, s_sem, r_sem, device):
        return pltpu.make_async_remote_copy(src_ref=src, dst_ref=dst, send_sem=s_sem, recv_sem=r_sem,
                                            device_id=device, device_id_type=MESH)

    def arrived(dst, r_sem):
        remote(dst, dst, w_send.at[0], r_sem, sib).wait_recv()

    def view(item, place):
        if item[0] == "S":
            slot, h = place[item[:3]], item[3]
            return bs.at[slot, halves[h]], w_recv.at[slot, h]
        return gt.at[item[1], lo_hi[item[2]]], g_recv.at[item[1], item[2]]

    def run(phase, finish=False):
        for x in range(NX):
            for k in (0, 1):

                @pl.when(jnp.logical_and(cx == x, core == k))
                def _(x=x, k=k):
                    place, n_sent, n_shared = places(x, k), 0, 0
                    ends = [-1.0, *phase_ends(x, k)]
                    for op in programs()[x, k]:
                        now = not finish and ends[phase] < op[0] <= ends[phase + 1]
                        if op[3] == "wait":
                            if now:
                                arrived(*view(op[4], place))
                        elif op[3] == "share":
                            part = bs.at[op[4]]
                            if now:
                                remote(part, part, s_send.at[n_shared], s_recv.at[op[4]], sib).start()
                            if finish:
                                remote(part, part, s_send.at[n_shared], s_recv.at[op[4]], sib).wait_send()
                            n_shared += 1
                        else:
                            _, _, _, _, item, kind, xd, there = op
                            dst, r_sem = view(there, places(xd, k))
                            if now:
                                remote(view(item, place)[0], dst, w_send.at[n_sent], r_sem, to[kind]).start()
                            if finish:
                                remote(view(item, place)[0], dst, w_send.at[n_sent], r_sem, to[kind]).wait_send()
                            n_sent += 1

    def shared(slot):
        arrived(bs.at[slot], s_recv.at[slot])

    run(0)

    gy = (0, 1, 3, 2) * 2
    gz = (0,) * 4 + (1,) * 4
    for g in range(8):
        row = vir[pl.ds(((zl + gz[g]) % NZL) * NY + (cy + gy[g]) % NY, 1), :]
        va[g] = jnp.broadcast_to(row, (nloc, nloc)).T
    vb = vir[pl.ds(narrow, 1), :]
    e_own = occ[omap[wide]]

    def block(q, g0, ng):
        pair = jnp.concatenate([bs[2 * q, 0:naux, :], bs[2 * q + 1, 0:naux, :]], axis=1)
        a = gt[g0 : g0 + ng].reshape(ng * nloc, naux)
        work[0 : ng * nloc, :] = jnp.dot(a, pair, preferred_element_type=F32)
        mine = bs[own, naux : naux + EXTRA, :].astype(F32)
        for k in range(2):
            j_off = jnp.where(q == 5, 6 - 11 * k, 2 * (q - 2) + k)
            e_sum = e_own + occ[omap[around(2 * chip - wide + j_off)]]
            delta = core - j_off
            theirs = bs[2 * q + k, naux : naux + EXTRA, :].astype(F32)
            pick = jnp.where(delta >= 0, mine, theirs)
            w = jnp.sum(jnp.where(rows16 == jnp.abs(delta), pick, 0.0), axis=0, keepdims=True)
            for g in range(g0, g0 + ng):
                v = work[(g - g0) * nloc : (g - g0 + 1) * nloc, k * nloc : (k + 1) * nloc]
                t = w * v / ((va[g] + vb) - e_sum)
                tt[pl.ds((2 * q + k) * nloc, nloc), COLUMN[g] * nloc : (COLUMN[g] + 1) * nloc] = t.T.astype(BF16)

    def pair_at(i):
        q = 0
        for x in range(NX):
            for j, value in enumerate(ORDER[x]):
                q = jnp.where(jnp.logical_and(cx == x, i == j), value, q)
        return q

    def blocks(first, last, g0, ng, wait=False):
        @pl.loop(first, last)
        def _(i):
            q = pair_at(i)
            if wait:
                shared(2 * q + 1 - core)
            block(q, g0, ng)

    run(1)
    blocks(0, 3, 0, 3, True)
    run(2)
    blocks(0, 3, 3, 2)
    blocks(3, 4, 0, 5, True)
    run(3)
    blocks(4, 5, 0, 5, True)
    run(4)
    blocks(0, 5, 5, 2)
    run(5)
    blocks(5, 6, 0, 7, True)
    y_rows = Y_ROWS
    z_rows = naux // 2 - y_rows

    def y_part(part):
        return pl.ds(pl.multiple_of(part * y_rows, 32), y_rows)

    def z_part(part):
        return pl.ds(pl.multiple_of(2 * y_rows + part * z_rows, 32), z_rows)

    def tile(p, rows):
        lhs = jnp.concatenate([bs[s, rows, :] for s in range(SLOTS)], axis=1)
        cols = pl.ds(pl.multiple_of(p * 2 * nloc, 2 * nloc), 2 * nloc)
        work[0 : rows.size, :] = jnp.dot(lhs, tt[:, cols], preferred_element_type=F32)

    def beside(way):
        return (wide, jnp.where(way == 0, right[1], left[1]))

    def y_copy(i, way):
        return remote(sy.at[i], ry.at[i], sy_sem.at[i], ry_sem.at[i], beside(way))

    def n_copy(i, device, rows):
        part = pl.ds(0, rows + EXTRA)
        return remote(sn.at[i, part], rn.at[i, part], sn_sem.at[i], rn_sem.at[i], device)

    def took_y(i):
        arrived(ry.at[i], ry_sem.at[i])
        return decode(ry.at[i], y_rows)

    def took_n(i, rows):
        part = rn.at[i, pl.ds(0, rows + EXTRA)]
        arrived(part, rn_sem.at[i])
        return decode(part, rows)

    def y_step(stage):
        @pl.loop(0, 2)
        def _(way):
            tile(3 if stage == 0 else 1 + way, y_part(1 - way if stage == 1 else way))
            value = work[0:y_rows, :]
            if stage == 2:
                value = value + took_y(way)
            encode(value, sy.at[2 * stage + way])
            y_copy(2 * stage + way, way).start()

    def z_step(p):
        @pl.loop(0, 2)
        def _(j):
            tile(p, z_part(j))
            keep[2 * p + j] = work[0:z_rows, 0:nloc]
            encode(work[0:z_rows, nloc : 2 * nloc], sn.at[2 * p + j])
            n_copy(2 * p + j, zpart, z_rows).start()

    def n_step(stage):
        @pl.loop(0, 2)
        def _(way):
            i = 6 + way if stage == 0 else 2 * (1 + way) + (1 - way if stage == 1 else way)
            value = keep[i] + took_n(i, z_rows)
            if stage == 2:
                value = value + took_n(8 + way, z_rows)
            encode(value, sn.at[8 + 2 * stage + way])
            n_copy(8 + 2 * stage + way, beside(way), z_rows).start()

    y_step(1)
    z_step(1)
    run(6)
    run(7)
    blocks(0, 6, 7, 1)
    y_step(0)
    z_step(3)
    z_step(2)
    y_step(2)
    n_step(0)
    z_step(0)
    n_step(1)

    @pl.loop(0, 2)
    def _(part):
        tile(0, y_part(part))
        total = work[0:y_rows, :] + took_y(4 - 2 * part) + took_y(3 + 2 * part)
        out[y_part(part), :] = total[:, 0:nloc]
        encode(total[:, nloc : 2 * nloc], sn.at[14 + part])
        n_copy(14 + part, zpart, y_rows).start()

    n_step(2)

    @pl.loop(0, 2)
    def _(j):
        out[z_part(j), :] = keep[j] + took_n(j, z_rows) + took_n(12 - 2 * j, z_rows) + took_n(11 + 2 * j, z_rows)

    @pl.loop(0, 2)
    def _(part):
        out[y_part(part), :] += took_n(14 + part, y_rows)

    run(0, True)

    @pl.loop(0, 6)
    def _(i):
        y_copy(i, i % 2).wait_send()

    @pl.loop(0, 14)
    def _(i):
        n_copy(i, sib, z_rows).wait_send()

    @pl.loop(14, 16)
    def _(i):
        n_copy(i, sib, y_rows).wait_send()


def per_device(three_index, orbital_map, occ_energy, vir_energy, pair_kept):
    _, naux, nloc = three_index.shape
    n_wide = lax.axis_size("wide")
    n_narrow = lax.axis_size("narrow")
    x = three_index.reshape(naux, nloc)
    kept = pair_kept.reshape(-1)
    vir = vir_energy.reshape(n_narrow, nloc)
    vmem = functools.partial(pl.BlockSpec, memory_space=pltpu.VMEM)
    smem = functools.partial(pl.BlockSpec, memory_space=pltpu.SMEM)
    hbm = functools.partial(pl.BlockSpec, memory_space=pl.ANY)
    dma = pltpu.SemaphoreType.DMA
    density = pl.pallas_call(
        functools.partial(kernel, n_wide, naux, nloc, kept.shape[0]),
        out_shape=jax.ShapeDtypeStruct((naux, nloc), F32),
        in_specs=[smem(), smem(), smem(), hbm(), vmem()],
        out_specs=vmem(),
        scratch_shapes=[
            pltpu.VMEM((SLOTS + RELAYS, naux + EXTRA, nloc), BF16),
            pltpu.VMEM((8, nloc, naux), BF16),
            pltpu.VMEM((8, nloc, nloc), F32),
            pltpu.VMEM((SLOTS * nloc, 8 * nloc), BF16),
            pltpu.VMEM((8 * nloc, 2 * nloc), F32),
            pltpu.VMEM((8, naux // 2 - Y_ROWS, nloc), F32),
            pltpu.VMEM((6, Y_ROWS + EXTRA, 2 * nloc), jnp.int16),
            pltpu.VMEM((6, Y_ROWS + EXTRA, 2 * nloc), jnp.int16),
            pltpu.VMEM((16, Y_ROWS + EXTRA, nloc), jnp.int16),
            pltpu.VMEM((16, Y_ROWS + EXTRA, nloc), jnp.int16),
            dma((1,)),
            dma((32,)),
            dma((SLOTS + RELAYS, 2)),
            dma((6,)),
            dma((SLOTS,)),
            dma((8, 2)),
            dma((6,)),
            dma((6,)),
            dma((16,)),
            dma((16,)),
        ],
        compiler_params=pltpu.CompilerParams(
            collective_id=0, has_side_effects=True, vmem_limit_bytes=60 * 1024 * 1024
        ),
    )(orbital_map, occ_energy, kept, x, vir)
    return density.reshape(1, naux, nloc)


def solution(mesh):
    placed = (P("wide", None, "narrow"), P(), P(), P(), P(None, "wide"))
    return jax.shard_map(
        per_device, mesh=mesh, in_specs=placed, out_specs=P("wide", None, "narrow"), check_vma=False
    )
```

```python
import collections
import functools
import heapq

import jax
import jax.numpy as jnp
from jax import lax
from jax.experimental import pallas as pl
from jax.experimental.pallas import tpu as pltpu
from jax.sharding import PartitionSpec as P

MESH = pl.DeviceIdType.MESH
F32 = jnp.float32
BF16 = jnp.bfloat16

NX, NY, NZL = 4, 4, 2
EXTRA = 16
Y_ROWS = 832
SLOTS = 12
LN2 = 0.6931471805599453
FINE = 64.0
TOP = 32000.0
COLUMN = (0, 2, 4, 6, 1, 3, 5, 7)

HOP = 0.2
ROUTES = {
    (3, 1): ((3, ((3, 0), (0, 1), (3, 2))), (3, ((3, 0), (3, 2), (2, 1)))),
    (3, 0): ((0, ((0, 1),)),),
    (2, 1): ((1, ((1, 0),)),),
    (2, 0): ((2, ((2, 1), (1, 0))),),
    (1, 1): ((0, ()), (1, ((1, 0),))),
}
ORDER = ((2, 3, 4, 5, 1, 0), (1, 2, 3, 4, 5, 0), (1, 2, 3, 0, 5, 4), (0, 1, 2, 5, 3, 4))
PHASES = ((3, 3), (4, 5), (5, 5), (5, 7), (6, 7), (6, 8))
RELAYS = 2


def slot_of(x, k, dz, owner):
    off = NX * dz + owner - x
    if -2 <= off <= 2:
        return 2 * (off + 2) + k
    if off == 3 and k == 0:
        return 10
    if off == -3 and k == 1:
        return 11
    return None


def messages():
    out = []

    def fw(k, xs, xd, dz, owner, h, rank=1):
        xs, xd, owner = xs % NX, xd % NX, owner % NX
        kind = "x+" if (xs + 1) % NX == xd else "x-"
        out.append((("S", dz, owner, h), kind, xs, xd, k, ("S", dz, owner, h), rank))

    for k in (0, 1):
        for x in range(NX):
            for h in (0, 1):
                fw(k, x, x + 1, 0, x, h, 2 + 0.1 * h)
                fw(k, x, x - 1, 0, x, 1 - h, 2 + 0.1 * h)
            fw(k, x + 1, x + 2, 0, x, 0)
            fw(k, x - 1, x - 2, 0, x, 1)
        for up in (True, False):
            kk, dz = (k, -1) if up else (1 - k, 1)

            def m(v, up=up):
                return v if up else NX - 1 - v

            for (owner, odd), ways in ROUTES.items():
                for h in (0, 1) if odd == k else ():
                    column, edges = ways[h * len(ways) // 2]
                    g = h if up else 1 - h
                    sent, got = ("S", 0, m(owner), g), ("S", dz, m(owner), g)
                    out.append((sent, "z+" if up else "z-", m(column), m(column), kk, got, 1))
                    for xs, xd in edges:
                        fw(kk, m(xs), m(xd), dz, m(owner), g, 0)
        for x in range(NX):

            def ag(g0, kind, g1, h, rank, k=k, x=x):
                out.append((("A", g0, h), kind, x, x, k, ("A", g1, h), rank))

            for h in (0, 1):
                ag(0, "zz", 4, h, 3 + 0.1 * h)
                ag(0, "y+", 2, h, 2 + 0.1 * h)
                ag(0, "y-", 1, 1 - h, 2 + 0.1 * h)
                ag(4, "y+", 6, h, 3)
                ag(4, "y-", 5, 1 - h, 3)
            ag(2, "y+", 3, 0, 1)
            ag(1, "y-", 3, 1, 1)
            ag(6, "y+", 7, 0, 1)
            ag(5, "y-", 7, 1, 1)
    return out


@functools.cache
def programs():
    ms = messages()
    devices = [(x, k) for x in range(NX) for k in (0, 1)]
    need, queues, flying, have, ready, clock = {}, {}, {}, {}, {}, 0.0
    for i, m in enumerate(ms):
        need.setdefault((m[2], m[4], m[0]), []).append(i)
    ops = {device: [(0.0, 9, 0, "share", 4 + device[1])] for device in devices}
    coming = [(0.0, x, k, z, item) for x, k in devices for z in (0, 1) for h in (0, 1)
              for item in (("S", 0, x, h), ("A", 0, h))]
    heapq.heapify(coming)
    while coming or flying:
        while coming and coming[0][0] <= clock + 1e-9:
            t, x, k, z, item = heapq.heappop(coming)
            have[x, k, item] = max(have.get((x, k, item), 0.0), t)
            for i in need.get((x, k, item), ()):
                kind = ("z-" if z else "z+") if ms[i][1] == "zz" else ms[i][1]
                heapq.heappush(queues.setdefault((kind, x, k, z), []), (t, ms[i][6], i, z))
                ready[i] = max(ready.get(i, 0.0), t)
        for key, queue in queues.items():
            if queue and key not in flying:
                _, _, i, z = heapq.heappop(queue)
                _, kind, x, *_ = ms[i]
                if kind == "zz":
                    links = [("even", "z-" if z else "z+", x)]
                elif kind in ("z+", "z-"):
                    links = [("even", kind, x), ("odd", kind, x)]
                else:
                    links = [(kind, x, z)]
                flying[key] = [i, z, 0.5, links]
        users = collections.Counter(link for flight in flying.values() for link in flight[3])
        rate = {key: min(1.0 / users[link] for link in flight[3]) for key, flight in flying.items()}
        step = min([flight[2] / rate[key] for key, flight in flying.items()], default=1e9)
        if coming:
            step = min(step, max(coming[0][0] - clock, 0.0))
        clock += step
        for key, flight in list(flying.items()):
            flight[2] -= rate[key] * step
            if flight[2] <= 1e-7:
                i, z, _, links = flying.pop(key)
                _, kind, _, xd, k, item, _ = ms[i]
                heapq.heappush(coming, (clock + HOP * len(links), xd, k, 1 - z if kind == "zz" else z, item))
    for i, (item, kind, xs, xd, k, item2, rank) in enumerate(ms):
        ops[xs, k].append((ready[i], rank, i, "send", item, kind, xd, item2))
        ops[xd, k].append((have[xd, k, item2], -1, i, "wait", item2))
    for (x, k), program in ops.items():
        for dz in (-1, 0, 1):
            for owner in range(NX):
                both = [have.get((x, k, ("S", dz, owner, h))) for h in (0, 1)]
                slot = slot_of(x, k, dz, owner)
                if slot is not None and slot != 4 + k:
                    program.append((max(both), 1, 0, "share", slot))
        program.sort(key=lambda op: op[:3])
    return ops


@functools.cache
def phase_ends(x, k):
    ends, end = [], 0.01
    for pairs, slices in PHASES:
        slots = [2 * q + c for q in ORDER[x][:pairs] for c in (0, 1)]
        for core in (0, 1):
            for op in programs()[x, core]:
                if op[3] == "share" and op[4] in slots:
                    end = max(end, op[0])
                if op[3] == "wait" and op[4][0] == "A" and core == k and op[4][1] < slices:
                    end = max(end, op[0])
        ends.append(end)
    return [0.01, *ends, 1000.0]


def places(x, k):
    found, spare = {}, SLOTS
    for op in programs()[x, k]:
        if op[3] == "wait" and op[4][0] == "S" and op[4][:3] not in found:
            slot = slot_of(x, k, op[4][1], op[4][2])
            if slot is None:
                slot, spare = spare, spare + 1
            found[op[4][:3]] = slot
    found["S", 0, x] = 4 + k
    assert spare <= SLOTS + RELAYS
    return found


def scale_of(level):
    return jnp.exp(level * (LN2 / FINE))


def encode(value, ref):
    rows = value.shape[0]
    top = jnp.maximum(jnp.max(jnp.abs(value), axis=0, keepdims=True), 1e-25)
    level = jnp.ceil(jnp.log(top) * (FINE / LN2))
    factor = TOP / scale_of(level)
    ref[0:rows, :] = jnp.round(value * factor).astype(jnp.int32).astype(jnp.int16)
    spread = jnp.broadcast_to(level, (EXTRA, value.shape[1]))
    ref[rows : rows + EXTRA, :] = spread.astype(jnp.int32).astype(jnp.int16)


def decode(ref, rows):
    level = ref[rows : rows + EXTRA, :].astype(jnp.int32).astype(F32)[0:1, :]
    return ref[0:rows, :].astype(jnp.int32).astype(F32) * (scale_of(level) * (1.0 / TOP))


def kernel(n_wide, naux, nloc, rounds, omap, occ, kept, x, vir, out, bs, gt, va, tt, work, keep, sy, ry, sn, rn,
           loc_sem, w_send, w_recv, s_send, s_recv, g_recv, sy_sem, ry_sem, sn_sem, rn_sem):
    wide = lax.axis_index("wide")
    narrow = lax.axis_index("narrow")
    core = wide % 2
    chip = wide // 2
    cx = chip % NX
    zh8 = wide - wide % (2 * NX)
    zl, cy = narrow // NY, narrow % NY

    def around(by):
        return (wide + by + n_wide) % n_wide

    def ringx(by):
        return zh8 + ((cx + by + NX) % NX) * 2 + core

    sib = (wide + 1 - 2 * core, narrow)
    right = (wide, zl * NY + (cy + 1) % NY)
    left = (wide, zl * NY + (cy + NY - 1) % NY)
    zpart = (wide, (1 - zl) * NY + cy)
    zup, zdown = (around(2 * NX), narrow), (around(-2 * NX), narrow)
    xup, xdown = (ringx(1), narrow), (ringx(-1), narrow)
    to = {"x+": xup, "x-": xdown, "z+": zup, "z-": zdown, "zz": zpart, "y+": right, "y-": left}

    half = naux // 2
    halves = (pl.ds(0, half), pl.ds(half, half + EXTRA))
    lo_hi = (pl.ds(0, nloc // 2), pl.ds(nloc // 2, nloc // 2))
    own = 4 + core

    local = [
        pltpu.make_async_copy(x, bs.at[own, pl.ds(0, naux)], loc_sem.at[0]),
    ]
    for c in local:
        c.start()
    barrier = pltpu.get_barrier_semaphore()
    greeted = [sib, *to.values()]
    for device in greeted:
        pl.semaphore_signal(barrier, inc=1, device_id=device, device_id_type=MESH)
    rows16 = lax.broadcasted_iota(jnp.int32, (EXTRA, nloc), 0)
    weights = jnp.zeros((EXTRA, nloc), F32)
    for r in range(rounds):
        weights = jnp.where(rows16 == r, kept[r].astype(F32), weights)
    bs[own, naux : naux + EXTRA, :] = weights.astype(BF16)
    for c in local:
        c.wait()
    for r in range(0, naux, nloc):
        gt[0, :, r : r + nloc] = bs[own, r : r + nloc, :].T
    pl.semaphore_wait(barrier, len(greeted))

    def remote(src, dst, s_sem, r_sem, device):
        return pltpu.make_async_remote_copy(src_ref=src, dst_ref=dst, send_sem=s_sem, recv_sem=r_sem,
                                            device_id=device, device_id_type=MESH)

    def arrived(dst, r_sem):
        remote(dst, dst, w_send.at[0], r_sem, sib).wait_recv()

    def view(item, place):
        if item[0] == "S":
            slot, h = place[item[:3]], item[3]
            return bs.at[slot, halves[h]], w_recv.at[slot, h]
        return gt.at[item[1], lo_hi[item[2]]], g_recv.at[item[1], item[2]]

    def run(phase, finish=False):
        for x in range(NX):
            for k in (0, 1):

                @pl.when(jnp.logical_and(cx == x, core == k))
                def _(x=x, k=k):
                    place, n_sent, n_shared = places(x, k), 0, 0
                    ends = [-1.0, *phase_ends(x, k)]
                    for op in programs()[x, k]:
                        now = not finish and ends[phase] < op[0] <= ends[phase + 1]
                        if op[3] == "wait":
                            if now:
                                arrived(*view(op[4], place))
                        elif op[3] == "share":
                            part = bs.at[op[4]]
                            if now:
                                remote(part, part, s_send.at[n_shared], s_recv.at[op[4]], sib).start()
                            if finish:
                                remote(part, part, s_send.at[n_shared], s_recv.at[op[4]], sib).wait_send()
                            n_shared += 1
                        else:
                            _, _, _, _, item, kind, xd, there = op
                            dst, r_sem = view(there, places(xd, k))
                            if now:
                                remote(view(item, place)[0], dst, w_send.at[n_sent], r_sem, to[kind]).start()
                            if finish:
                                remote(view(item, place)[0], dst, w_send.at[n_sent], r_sem, to[kind]).wait_send()
                            n_sent += 1

    def shared(slot):
        arrived(bs.at[slot], s_recv.at[slot])

    run(0)

    gy = (0, 1, 3, 2) * 2
    gz = (0,) * 4 + (1,) * 4
    for g in range(8):
        row = vir[pl.ds(((zl + gz[g]) % NZL) * NY + (cy + gy[g]) % NY, 1), :]
        va[g] = jnp.broadcast_to(row, (nloc, nloc)).T
    vb = vir[pl.ds(narrow, 1), :]
    e_own = occ[omap[wide]]

    def block(q, g0, ng):
        pair = jnp.concatenate([bs[2 * q, 0:naux, :], bs[2 * q + 1, 0:naux, :]], axis=1)
        a = gt[g0 : g0 + ng].reshape(ng * nloc, naux)
        work[0 : ng * nloc, :] = jnp.dot(a, pair, preferred_element_type=F32)
        mine = bs[own, naux : naux + EXTRA, :].astype(F32)
        for k in range(2):
            j_off = jnp.where(q == 5, 6 - 11 * k, 2 * (q - 2) + k)
            e_sum = e_own + occ[omap[around(2 * chip - wide + j_off)]]
            delta = core - j_off
            theirs = bs[2 * q + k, naux : naux + EXTRA, :].astype(F32)
            pick = jnp.where(delta >= 0, mine, theirs)
            w = jnp.sum(jnp.where(rows16 == jnp.abs(delta), pick, 0.0), axis=0, keepdims=True)
            for g in range(g0, g0 + ng):
                v = work[(g - g0) * nloc : (g - g0 + 1) * nloc, k * nloc : (k + 1) * nloc]
                t = w * v / ((va[g] + vb) - e_sum)
                tt[pl.ds((2 * q + k) * nloc, nloc), COLUMN[g] * nloc : (COLUMN[g] + 1) * nloc] = t.T.astype(BF16)

    def pair_at(i):
        q = 0
        for x in range(NX):
            for j, value in enumerate(ORDER[x]):
                q = jnp.where(jnp.logical_and(cx == x, i == j), value, q)
        return q

    def blocks(first, last, g0, ng, wait=False):
        @pl.loop(first, last)
        def _(i):
            q = pair_at(i)
            if wait:
                shared(2 * q + 1 - core)
            block(q, g0, ng)

    run(1)
    blocks(0, 3, 0, 3, True)
    run(2)
    blocks(0, 3, 3, 2)
    blocks(3, 4, 0, 5, True)
    run(3)
    blocks(4, 5, 0, 5, True)
    run(4)
    blocks(0, 5, 5, 2)
    run(5)
    blocks(5, 6, 0, 7, True)
    y_rows = Y_ROWS
    z_rows = naux // 2 - y_rows

    def y_part(part):
        return pl.ds(pl.multiple_of(part * y_rows, 32), y_rows)

    def z_part(part):
        return pl.ds(pl.multiple_of(2 * y_rows + part * z_rows, 32), z_rows)

    def tile(p, rows):
        lhs = jnp.concatenate([bs[s, rows, :] for s in range(SLOTS)], axis=1)
        cols = pl.ds(pl.multiple_of(p * 2 * nloc, 2 * nloc), 2 * nloc)
        work[0 : rows.size, :] = jnp.dot(lhs, tt[:, cols], preferred_element_type=F32)

    def beside(way):
        return (wide, jnp.where(way == 0, right[1], left[1]))

    def y_copy(i, way):
        return remote(sy.at[i], ry.at[i], sy_sem.at[i], ry_sem.at[i], beside(way))

    def n_copy(i, device, rows):
        part = pl.ds(0, rows + EXTRA)
        return remote(sn.at[i, part], rn.at[i, part], sn_sem.at[i], rn_sem.at[i], device)

    def took_y(i):
        arrived(ry.at[i], ry_sem.at[i])
        return decode(ry.at[i], y_rows)

    def took_n(i, rows):
        part = rn.at[i, pl.ds(0, rows + EXTRA)]
        arrived(part, rn_sem.at[i])
        return decode(part, rows)

    def y_step(stage):
        @pl.loop(0, 2)
        def _(way):
            tile(3 if stage == 0 else 1 + way, y_part(1 - way if stage == 1 else way))
            value = work[0:y_rows, :]
            if stage == 2:
                value = value + took_y(way)
            encode(value, sy.at[2 * stage + way])
            y_copy(2 * stage + way, way).start()

    def z_step(p):
        @pl.loop(0, 2)
        def _(j):
            tile(p, z_part(j))
            keep[2 * p + j] = work[0:z_rows, 0:nloc]
            encode(work[0:z_rows, nloc : 2 * nloc], sn.at[2 * p + j])
            n_copy(2 * p + j, zpart, z_rows).start()

    def n_step(stage):
        @pl.loop(0, 2)
        def _(way):
            i = 6 + way if stage == 0 else 2 * (1 + way) + (1 - way if stage == 1 else way)
            value = keep[i] + took_n(i, z_rows)
            if stage == 2:
                value = value + took_n(8 + way, z_rows)
            encode(value, sn.at[8 + 2 * stage + way])
            n_copy(8 + 2 * stage + way, beside(way), z_rows).start()

    y_step(1)
    z_step(1)
    run(6)
    run(7)
    blocks(0, 6, 7, 1)
    y_step(0)
    z_step(3)
    z_step(2)
    z_step(0)
    y_step(2)
    n_step(0)
    n_step(1)

    @pl.loop(0, 2)
    def _(part):
        tile(0, y_part(part))
        total = work[0:y_rows, :] + took_y(4 - 2 * part) + took_y(3 + 2 * part)
        out[y_part(part), :] = total[:, 0:nloc]
        encode(total[:, nloc : 2 * nloc], sn.at[14 + part])
        n_copy(14 + part, zpart, y_rows).start()

    n_step(2)

    @pl.loop(0, 2)
    def _(j):
        out[z_part(j), :] = keep[j] + took_n(j, z_rows) + took_n(12 - 2 * j, z_rows) + took_n(11 + 2 * j, z_rows)

    @pl.loop(0, 2)
    def _(part):
        out[y_part(part), :] += took_n(14 + part, y_rows)

    run(0, True)

    @pl.loop(0, 6)
    def _(i):
        y_copy(i, i % 2).wait_send()

    @pl.loop(0, 14)
    def _(i):
        n_copy(i, sib, z_rows).wait_send()

    @pl.loop(14, 16)
    def _(i):
        n_copy(i, sib, y_rows).wait_send()


def per_device(three_index, orbital_map, occ_energy, vir_energy, pair_kept):
    _, naux, nloc = three_index.shape
    n_wide = lax.axis_size("wide")
    n_narrow = lax.axis_size("narrow")
    x = three_index.reshape(naux, nloc)
    kept = pair_kept.reshape(-1)
    vir = vir_energy.reshape(n_narrow, nloc)
    vmem = functools.partial(pl.BlockSpec, memory_space=pltpu.VMEM)
    smem = functools.partial(pl.BlockSpec, memory_space=pltpu.SMEM)
    hbm = functools.partial(pl.BlockSpec, memory_space=pl.ANY)
    dma = pltpu.SemaphoreType.DMA
    density = pl.pallas_call(
        functools.partial(kernel, n_wide, naux, nloc, kept.shape[0]),
        out_shape=jax.ShapeDtypeStruct((naux, nloc), F32),
        in_specs=[smem(), smem(), smem(), hbm(), vmem()],
        out_specs=vmem(),
        scratch_shapes=[
            pltpu.VMEM((SLOTS + RELAYS, naux + EXTRA, nloc), BF16),
            pltpu.VMEM((8, nloc, naux), BF16),
            pltpu.VMEM((8, nloc, nloc), F32),
            pltpu.VMEM((SLOTS * nloc, 8 * nloc), BF16),
            pltpu.VMEM((8 * nloc, 2 * nloc), F32),
            pltpu.VMEM((8, naux // 2 - Y_ROWS, nloc), F32),
            pltpu.VMEM((6, Y_ROWS + EXTRA, 2 * nloc), jnp.int16),
            pltpu.VMEM((6, Y_ROWS + EXTRA, 2 * nloc), jnp.int16),
            pltpu.VMEM((16, Y_ROWS + EXTRA, nloc), jnp.int16),
            pltpu.VMEM((16, Y_ROWS + EXTRA, nloc), jnp.int16),
            dma((1,)),
            dma((32,)),
            dma((SLOTS + RELAYS, 2)),
            dma((6,)),
            dma((SLOTS,)),
            dma((8, 2)),
            dma((6,)),
            dma((6,)),
            dma((16,)),
            dma((16,)),
        ],
        compiler_params=pltpu.CompilerParams(
            collective_id=0, has_side_effects=True, vmem_limit_bytes=60 * 1024 * 1024
        ),
    )(orbital_map, occ_energy, kept, x, vir)
    return density.reshape(1, naux, nloc)


def solution(mesh):
    placed = (P("wide", None, "narrow"), P(), P(), P(), P(None, "wide"))
    return jax.shard_map(
        per_device, mesh=mesh, in_specs=placed, out_specs=P("wide", None, "narrow"), check_vma=False
    )
```
